1024 devices in a mesh: map: 128 (over z, y_lo, core), layer: 8 (over x, y_hi).
Axes of the slice: x: 4, y: 8 (y_hi: 2, y_lo: 4; y = y_hi * 4 + y_lo), z: 16, core: 2. Of those that a mesh axis runs over, the one named last changes fastest.
Arguments:
- velocity_init: float32 [2, 32, 256, 2048], P(None, 'layer', 'map'), may hold values from -4 to 4
- driving: float32 [2, 256, 2048], P(None, 'map', 'layer'), may hold values from -80 to 80
- observed: float32 [2, 256, 2048], P(None, 'map', 'layer'), may hold values from -4 to 4
- log_friction: float32 [256, 2048], P('map', 'layer'), may hold values from -1 to 1.5
- ice_mask: int32 [256, 2048], P('map', 'layer'), may hold values from 0 to 2
Outputs:
- velocity: float32 [2, 32, 256, 2048], P(None, 'layer', 'map')
- friction_new: float32 [256, 2048], P('map', 'layer')
- misfit: float32 [], replicated
The draws below stay inside these ranges and needn't reach their ends.
All inputs are finite; a program needn't handle non-finite values.
Results may differ from the reference program's by a relative error of at most 0.0003.
Values sent between devices are 32-bit elements; how exact they have to be, the bound alone decides.
A program may use at most 32 MiB of HBM per device.

```python
import math
import jax
import jax.numpy as jnp
from jax import lax

NX = 256
NY = 2048
NZ = 32


def draw_driving(key, part):
    keys = jax.random.split(key, 3)
    base = jnp.clip(jax.random.normal(keys[0], (2, NX, NY), jnp.float32), -5.0, 5.0)
    row_scale = jnp.exp(jax.random.uniform(keys[1], (1, NX, 1), jnp.float32) * math.log(10.0))
    col_scale = jnp.exp(jax.random.uniform(keys[2], (1, 1, NY), jnp.float32) * math.log(10.0))
    trend = 1.0 + 2.0 * jnp.arange(NX, dtype=jnp.float32)[None, :, None] / NX
    return 0.05 * base * row_scale * col_scale * trend


def place_ends(entries, rng, smallest, largest):
    place = [jax.random.randint(jax.random.fold_in(rng, axis), (), 0, length) for axis, length in enumerate(entries.shape)]
    main_axis = entries.shape.index(max(entries.shape))
    next_to = place[:main_axis] + [(place[main_axis] + 1) % entries.shape[main_axis]] + place[main_axis + 1:]
    return entries.at[tuple(place)].set(smallest).at[tuple(next_to)].set(largest)


def block_levels(stream_key, shape, cuts, smallest, high):
    factor_of, own = 1.0, jax.random.fold_in(stream_key, 6)
    for axis_at, blocks in cuts:
        draws = jnp.exp(jax.random.uniform(jax.random.fold_in(own, axis_at), (blocks,), jnp.float32, smallest / len(cuts), high / len(cuts)))
        factor_of = factor_of * jnp.repeat(draws, shape[axis_at] // blocks).reshape([-1 if axis == axis_at else 1 for axis in range(len(shape))])
    return factor_of


def normal_values(own_key, extent, width, bound, shards=(), kind=jnp.bfloat16):
    level = block_levels(own_key, extent, shards, -0.22, 0.18) if shards else 1.0
    entries = jax.random.normal(own_key, extent, jnp.float32) * width * level
    return jnp.minimum(jnp.maximum(entries, -bound), bound).astype(kind)


def setup_inputs(seed: int = 0) -> dict:
    key_of = jax.random.split(jax.random.key(seed), 6)
    velocity_init = normal_values(key_of[0], (2, NZ, NX, NY), 0.5, 4.0, ((1, 8), (2, 128)), jnp.float32)
    driving = draw_driving(jax.random.fold_in(key_of[5], 71), 0)
    observed = normal_values(key_of[2], (2, NX, NY), 0.5, 4.0, ((1, 128), (2, 8)), jnp.float32)
    log_friction = jnp.clip(-1.0 + 2.5 * jax.random.uniform(key_of[3], (NX, NY), jnp.float32) ** block_levels(key_of[3], (NX, NY), ((0, 128), (1, 8)), -0.2, 0.2), -1.0, 1.5)
    ice_mask = place_ends(jax.random.randint(key_of[4], (NX, NY), 0, 3), jax.random.fold_in(key_of[4], 1), 0, 2).astype(jnp.int32)
    return {"velocity_init": velocity_init, "driving": driving, "observed": observed, "log_friction": log_friction, "ice_mask": ice_mask}


strain_floor = 0.1
step_size = 0.5

def viscosity_of(extended):
    along_x = extended[0]
    along_y = extended[1]
    stretch_x = (along_x[:, 2:, 1:-1] - along_x[:, :-2, 1:-1]) * 0.5
    shear_uy = (along_x[:, 1:-1, 2:] - along_x[:, 1:-1, :-2]) * 0.5
    shear_vx = (along_y[:, 2:, 1:-1] - along_y[:, :-2, 1:-1]) * 0.5
    stretch_y = (along_y[:, 1:-1, 2:] - along_y[:, 1:-1, :-2]) * 0.5
    shearing = shear_uy + shear_vx
    strain_rate = stretch_x * stretch_x + stretch_y * stretch_y + stretch_x * stretch_y + 0.25 * shearing * shearing
    return jnp.power(strain_floor + strain_rate, -1.0 / 3.0)

def face_terms(viscous):
    centre = viscous[:, 1:-1, 1:-1]
    east_face = 0.5 * (centre + viscous[:, 2:, 1:-1])
    west_face = 0.5 * (centre + viscous[:, :-2, 1:-1])
    north_face = 0.5 * (centre + viscous[:, 1:-1, 2:])
    south_face = 0.5 * (centre + viscous[:, 1:-1, :-2])
    return (east_face, west_face, north_face, south_face)

def horizontal_diag(face_list):
    east_face, west_face, north_face, south_face = face_list
    first = 4.0 * (east_face + west_face) + (north_face + south_face)
    second = east_face + west_face + 4.0 * (north_face + south_face)
    return jnp.stack([first, second], 0)

def neighbour_sum(face_list, extended):
    east_face, west_face, north_face, south_face = face_list
    comp_u = extended[0]
    comp_v = extended[1]
    first = 4.0 * (east_face * comp_u[:, 2:, 1:-1] + west_face * comp_u[:, :-2, 1:-1]) + north_face * comp_u[:, 1:-1, 2:] + south_face * comp_u[:, 1:-1, :-2]
    second = east_face * comp_v[:, 2:, 1:-1] + west_face * comp_v[:, :-2, 1:-1] + 4.0 * (north_face * comp_v[:, 1:-1, 2:] + south_face * comp_v[:, 1:-1, :-2])
    return jnp.stack([first, second], 0)

def column_solve(centre, side_diag, right_hand, friction):
    layer_total = centre.shape[0]
    vertical_gain = 2.0 * float(layer_total * layer_total)
    coupling = vertical_gain * 0.5 * (centre[:-1] + centre[1:])
    zero_layer = jnp.zeros_like(centre[:1])
    lower_link = jnp.concatenate([zero_layer, coupling], 0)
    upper_link = jnp.concatenate([coupling, zero_layer], 0)
    bed_term = jnp.concatenate([friction[None], jnp.zeros_like(centre[1:])], 0)
    diagonal = (lower_link + upper_link + bed_term)[None] + side_diag
    diagonal = jnp.moveaxis(diagonal, 1, 0)
    right_side = jnp.moveaxis(right_hand, 1, 0)

    def forward(carried, layer_item):
        ratio_prev, value_prev = carried
        diag_layer, lower_layer, upper_layer, right_layer = layer_item
        pivots = diag_layer + lower_layer * ratio_prev
        ratio = -upper_layer / pivots
        value = (right_layer + lower_layer * value_prev) / pivots
        return ((ratio, value), (ratio, value))
    start = (jnp.zeros_like(right_side[0]), jnp.zeros_like(right_side[0]))
    final_pair, (ratios, values) = lax.scan(forward, start, (diagonal, lower_link, upper_link, right_side), unroll=8)

    def backward(following, layer_item):
        ratio, value = layer_item
        current = value - ratio * following
        return (current, current)
    final_row, solved = lax.scan(backward, jnp.zeros_like(right_side[0]), (ratios, values), reverse=True, unroll=8)
    return jnp.moveaxis(solved, 0, 1)

def top_source(mismatch, layer_count):
    zero_part = jnp.zeros((2, layer_count - 1) + mismatch.shape[1:], jnp.float32)
    return jnp.concatenate([zero_part, (float(layer_count) * mismatch)[:, None]], 1)

def reference(velocity_init, driving, observed, log_friction, ice_mask):
    ice_cols = ice_mask != 0
    friction = jnp.exp(log_friction) * (ice_mask == 1).astype(jnp.float32)
    forcing = driving[:, None]
    velocity = velocity_init
    for iteration in range(2):
        padded = jnp.pad(velocity, ((0, 0), (0, 0), (2, 2), (2, 2)))
        viscous = viscosity_of(padded)
        face_list = face_terms(viscous)
        centre = viscous[:, 1:-1, 1:-1]
        side_diag = horizontal_diag(face_list)
        side_sum = neighbour_sum(face_list, padded[:, :, 1:-1, 1:-1])
        velocity = jnp.where(ice_cols, column_solve(centre, side_diag, forcing + side_sum, friction), 0.0)
    mismatch = jnp.where(ice_cols, velocity[:, -1] - observed, 0.0)
    source = top_source(mismatch, velocity.shape[1])
    adjoint = jnp.where(ice_cols, column_solve(centre, side_diag, source, friction), 0.0)
    adjoint_rim = jnp.pad(adjoint, ((0, 0), (0, 0), (1, 1), (1, 1)))
    adjoint = jnp.where(ice_cols, column_solve(centre, side_diag, source + neighbour_sum(face_list, adjoint_rim), friction), 0.0)
    gradient = -friction * (velocity[0, 0] * adjoint[0, 0] + velocity[1, 0] * adjoint[1, 0])
    column_count = NX * NY
    misfit = 0.5 * jnp.sum(mismatch * mismatch) / column_count
    grad_scale = jnp.sqrt(jnp.sum(gradient * gradient) / column_count + 1e-06)
    return (velocity, log_friction - step_size * gradient / grad_scale, misfit)
```

```python
import jax
import jax.numpy as jnp
from jax import lax
from jax.experimental import pallas as pl
from jax.experimental.pallas import tpu as pltpu
from jax.sharding import PartitionSpec as P

strain_floor = 0.1
step_size = 0.5
LAYERS = 32
SLOTS = 8
BLOCKS = 128
GROUPS = 4
COLUMNS = 256 * 2048
MESH = pl.DeviceIdType.MESH
f32 = jnp.float32


def place(m):
    return lax.div(m, 8), lax.rem(lax.div(m, 2), 4), lax.rem(m, 2)


def device_at(x, y, z, core):
    return ((z * 4 + lax.rem(y, 4)) * 2 + core, x * 2 + lax.div(y, 4))


def owner_of(m, l):
    z, y_lo, core = place(m)
    y = lax.rem(l, 2) * 4 + y_lo
    odd = lax.rem(z, 2)
    return device_at(lax.div(l, 2), lax.rem((1 - odd) * (y + 2) + odd * (13 - y), 8), z, core)


def block_of(x, y, z, core):
    odd = lax.rem(z, 2)
    return device_at(x, lax.rem((1 - odd) * (y + 6) + odd * (13 - y), 8), z, core)


def kernel(
    vel_hbm, drv_hbm, obs_hbm, logf_hbm, mask_hbm,
    out_hbm, fric_out, misfit_out,
    vin, drv, obs, logf, mask, stage_main, stage_rim, small, small_in,
    w0m, w0r, w1m, w1r, w2m, w2r, dnm, dnr, upm, upr, dnm1, dnr1, upm1, upr1,
    am, ar, adn, aup,
    eta_m, eta_r, diag_m, diag_r, rhs_m, rhs_r, ratio_m, ratio_r, val_m, val_r, inv_m, inv_r, rim_x, faces,
    vel_in, vout, grad, grad_in,
    row1, row2, row3, sum1, sum2, sum3,
    load_sem, out_sem, a2a_send, a2a_recv, small_send, small_recv, halo_send, halo_recv,
    vel_send, vel_recv, grad_send, grad_recv,
    s1_send, s1_recv, s2_send, s2_recv, s3_send, s3_recv,
):
    M = lax.axis_index("map")
    L = lax.axis_index("layer")
    z, y_lo, core = place(M)
    x = lax.div(L, 2)
    y = lax.rem(L, 2) * 4 + y_lo
    bm, bl = block_of(x, y, z, core)
    below = owner_of(lax.rem(bm + BLOCKS - 1, BLOCKS), bl)
    above = owner_of(lax.rem(bm + 1, BLOCKS), bl)
    owners = [owner_of(M, jnp.int32(l)) for l in range(SLOTS)]
    holders = [(bm, jnp.int32(l)) for l in range(SLOTS)]
    me1, me2, me3 = x * 2 + core, y, z

    def peer1(j):
        return device_at(lax.div(j, 2), y, z, lax.rem(j, 2))

    def peer2(j):
        return device_at(x, j, z, core)

    def peer3(j):
        return device_at(x, y, j, core)

    stages = (
        (8, me1, peer1, row1, sum1, s1_send, s1_recv),
        (8, me2, peer2, row2, sum2, s2_send, s2_recv),
        (16, me3, peer3, row3, sum3, s3_send, s3_recv),
    )
    partners = []
    for count, me, peer, *_ in reversed(stages):
        partners += [peer(lax.rem(me + i, count)) for i in range(1, count)]
    partners += owners + holders + [below, above]
    barrier = pltpu.get_barrier_semaphore()
    for partner in partners:
        pl.semaphore_signal(barrier, inc=1, device_id=partner, device_id_type=MESH)

    loads = [
        pltpu.make_async_copy(src, dst, load_sem.at[i])
        for i, (src, dst) in enumerate(
            ((vel_hbm, vin), (drv_hbm, drv), (obs_hbm, obs), (logf_hbm, logf), (mask_hbm, mask))
        )
    ]
    for load in loads:
        load.start()
    for load in loads[1:]:
        load.wait()
    small[0:8, :] = drv[...]
    small[8:16, :] = obs[...]
    small[16:20, :] = jnp.exp(logf[...]) * (mask[...] == 1).astype(f32)
    small[20:24, :] = (mask[...] != 0).astype(f32)
    loads[0].wait()

    lane2 = lax.broadcasted_iota(jnp.int32, (2, 128), 1)
    zero2 = jnp.zeros((2, 128), f32)
    for c in range(2):
        for kk in range(4):
            base = (c * 4 + kk) * 32
            for l in range(SLOTS):
                at = l * 32 + kk * 8 + c * 4
                stage_main[at:at + 4, :] = vin[base + l * 4:base + l * 4 + 4, :]
                right = vin[base + l * 4 + 4:base + l * 4 + 6, :] if l < SLOTS - 1 else zero2
                left = vin[base + l * 4 - 2:base + l * 4, :] if l > 0 else zero2
                at = l * 16 + kk * 4 + c * 2
                stage_rim[at:at + 2, :] = jnp.where(lane2 < 64, right, left)

    pl.semaphore_wait(barrier, len(partners))

    sends = []

    def remote(src, dst, send_sem, recv_sem, device):
        copy = pltpu.make_async_remote_copy(
            src_ref=src, dst_ref=dst, send_sem=send_sem, recv_sem=recv_sem, device_id=device, device_id_type=MESH
        )
        copy.start()
        sends.append(copy)

    def arrived(ref, sem):
        pltpu.make_async_copy(ref, ref, sem).wait()

    rows_main = pl.ds(pl.multiple_of(L * 32, 32), 32)
    rows_rim = pl.ds(pl.multiple_of(L * 16, 16), 16)
    for l in range(SLOTS):
        remote(stage_main.at[l * 32:l * 32 + 32], w0m.at[rows_main], a2a_send.at[0, l], a2a_recv.at[0, L], owners[l])
        remote(stage_rim.at[l * 16:l * 16 + 16], w0r.at[rows_rim], a2a_send.at[1, l], a2a_recv.at[1, L], owners[l])
    for side in range(3):
        target = owner_of(M, lax.rem(L + SLOTS + 1 - side, SLOTS))
        remote(small, small_in.at[side], small_send.at[side], small_recv.at[side], target)

    for l in range(SLOTS):
        rm, rr = pl.ds(l * 32, 32), pl.ds(l * 16, 16)
        arrived(w0m.at[rm], a2a_recv.at[0, l])
        arrived(w0r.at[rr], a2a_recv.at[1, l])
        for i, (device, mains, rims) in enumerate(((below, upm, upr), (above, dnm, dnr))):
            for part, src, dst, rows in ((0, w0m, mains, rm), (1, w0r, rims, rr)):
                pltpu.make_async_remote_copy(
                    src_ref=src.at[rows], dst_ref=dst.at[rows], send_sem=halo_send.at[0, i, part],
                    recv_sem=halo_recv.at[0, i, part], device_id=device, device_id_type=MESH,
                ).start()

    for side in range(3):
        arrived(small_in.at[side], small_recv.at[side])
    lane4 = lax.broadcasted_iota(jnp.int32, (4, 128), 1)
    lane8 = lax.broadcasted_iota(jnp.int32, (8, 128), 1)
    has_left = (bl > 0).astype(f32)
    has_right = (bl < SLOTS - 1).astype(f32)
    has_below = (bm > 0).astype(f32)
    has_above = (bm < BLOCKS - 1).astype(f32)

    def double(rows):
        return jnp.concatenate([rows, rows], 0)

    def rim_rows(start, comps):
        parts = []
        for c in range(comps):
            at = start + 4 * c
            parts.append(jnp.where(lane2 < 64, small_in[2, at:at + 2, :] * has_right, small_in[0, at + 2:at + 4, :] * has_left))
        if comps == 1:
            parts = parts * 2
        return double(jnp.concatenate(parts, 0))

    drive = (small_in[1, 0:8, :], rim_rows(0, 2))
    seen = (small_in[1, 8:16, :], rim_rows(8, 2))
    bed = (double(small_in[1, 16:20, :]), rim_rows(16, 1))
    ice = (double(small_in[1, 20:24, :]) > 0.5, rim_rows(20, 1) > 0.5)

    def ahead(tiles):
        turned = [pltpu.roll(t, 127, 1) for t in tiles]
        return [jnp.where(lane8 == 127, turned[(i + 1) % 3], turned[i]) for i in range(3)]

    def behind(tiles):
        turned = [pltpu.roll(t, 1, 1) for t in tiles]
        return [jnp.where(lane8 == 0, turned[(i + 2) % 3], turned[i]) for i in range(3)]

    def load_tiles(main, rim, j, c, r):
        tiles = [main[pl.ds(j * 64 + (c * 4 + t * 2 + r), 8, stride=8), :] for t in range(2)]
        return tiles + [rim[pl.ds(j * 32 + (c * 2 + r), 8, stride=4), :]]

    def store_tile(main, rim, j, c, t, r, value):
        if t < 2:
            main[pl.ds(j * 64 + (c * 4 + t * 2 + r), 8, stride=8), :] = value
        else:
            rim[pl.ds(j * 64 + (c * 2 + r), 8, stride=8), :] = value

    def scaled(tiles, factor):
        return [t * factor for t in tiles]

    def forward_terms(own, low, high):
        def group(j, carry):
            w = []
            for c in range(2):
                rows = [scaled(load_tiles(*low, j, c, r), has_below) for r in range(2)]
                rows += [load_tiles(*own, j, c, r) for r in range(2)]
                rows += [scaled(load_tiles(*high, j, c, r), has_above) for r in range(2)]
                w.append(rows)
            right = [[ahead(w[c][r]) for r in range(1, 5)] for c in range(2)]
            left = [[behind(w[c][r]) for r in range(1, 5)] for c in range(2)]
            eta = []
            for r in range(4):
                tiles = []
                for t in range(3):
                    u_x = (w[0][r + 2][t] - w[0][r][t]) * 0.5
                    v_x = (w[1][r + 2][t] - w[1][r][t]) * 0.5
                    u_y = (right[0][r][t] - left[0][r][t]) * 0.5
                    v_y = (right[1][r][t] - left[1][r][t]) * 0.5
                    shear = u_y + v_x
                    rate = u_x * u_x + v_y * v_y + u_x * v_y + 0.25 * shear * shear
                    tiles.append(jnp.exp(jnp.log(strain_floor + rate) * (-1.0 / 3.0)))
                eta.append(tiles)
            for r in range(2):
                eta_right, eta_left = ahead(eta[r + 1]), behind(eta[r + 1])
                for t in range(3):
                    centre = eta[r + 1][t]
                    east = 0.5 * (centre + eta[r + 2][t])
                    west = 0.5 * (centre + eta[r][t])
                    north = 0.5 * (centre + eta_right[t])
                    south = 0.5 * (centre + eta_left[t])
                    along, across = east + west, north + south
                    if t < 2:
                        for i, face in enumerate((east, west, north, south)):
                            faces[j, (r * 2 + t) * 4 + i] = face
                    u, v = w
                    sum_u = (
                        4.0 * (east * u[r + 3][t] + west * u[r + 1][t])
                        + north * right[0][r + 1][t] + south * left[0][r + 1][t]
                    )
                    sum_v = (
                        east * v[r + 3][t] + west * v[r + 1][t]
                        + 4.0 * (north * right[1][r + 1][t] + south * left[1][r + 1][t])
                    )
                    store_tile(eta_m, eta_r, j, 0, t, r, centre)
                    store_tile(eta_m, eta_r, j, 1, t, r, centre)
                    store_tile(diag_m, diag_r, j, 0, t, r, 4.0 * along + across)
                    store_tile(diag_m, diag_r, j, 1, t, r, along + 4.0 * across)
                    store_tile(rhs_m, rhs_r, j, 0, t, r, sum_u)
                    store_tile(rhs_m, rhs_r, j, 1, t, r, sum_v)
            return carry

        lax.fori_loop(0, GROUPS, group, 0)

    pairs = (
        (eta_m, diag_m, rhs_m, ratio_m, val_m, inv_m),
        (eta_r, diag_r, rhs_r, ratio_r, val_r, inv_r),
    )

    def at(k):
        return pl.ds(pl.multiple_of(k * 8, 8), 8)

    def solve(out_main):
        def eliminate(k, carry, last=False):
            new = []
            for part in range(2):
                eta, diag, rhs, ratio, val, inv = pairs[part]
                lower, ratio_prev, val_prev, pad = carry[part]
                if last:
                    upper = jnp.zeros((8, 128), f32)
                else:
                    upper = 1024.0 * (eta[at(k), :] + eta[at(k + 1), :])
                inverse = 1.0 / (((lower + upper + pad) + diag[at(k), :]) + lower * ratio_prev)
                ratio_now = -upper * inverse
                val_now = (drive[part] + rhs[at(k), :] + lower * val_prev) * inverse
                ratio[at(k), :] = ratio_now
                val[at(k), :] = val_now
                inv[at(k), :] = inverse
                new.append((upper, ratio_now, val_now, jnp.zeros((8, 128), f32)))
            return tuple(new)

        zero = jnp.zeros((8, 128), f32)
        carry = tuple((zero, zero, zero, bed[part]) for part in range(2))
        carry = lax.fori_loop(0, LAYERS - 1, eliminate, carry)
        eliminate(LAYERS - 1, carry, last=True)
        outs = (out_main, rim_x)

        def substitute(i, following):
            k = LAYERS - 1 - i
            new = []
            for part in range(2):
                ratio, val = pairs[part][3], pairs[part][4]
                now = val[at(k), :] - ratio[at(k), :] * following[part]
                outs[part][at(k), :] = jnp.where(ice[part], now, 0.0)
                new.append(now)
            return tuple(new)

        lax.fori_loop(0, LAYERS, substitute, (zero, zero))

    def squeeze_rim(out_rim):
        for s in range(4):
            for j in range(GROUPS):
                out_rim[pl.ds(j * 32 + s, 8, stride=4), :] = rim_x[pl.ds(j * 64 + s, 8, stride=8), :]

    for i, (mains, rims) in enumerate(((upm, upr), (dnm, dnr))):
        arrived(mains, halo_recv.at[0, i, 0])
        arrived(rims, halo_recv.at[0, i, 1])
    forward_terms((w0m, w0r), (dnm, dnr), (upm, upr))
    solve(w1m)
    squeeze_rim(w1r)
    for i, (device, mains, rims) in enumerate(((below, upm1, upr1), (above, dnm1, dnr1))):
        remote(w1m, mains, halo_send.at[1, i, 0], halo_recv.at[1, i, 0], device)
        remote(w1r, rims, halo_send.at[1, i, 1], halo_recv.at[1, i, 1], device)

    for i, (mains, rims) in enumerate(((upm1, upr1), (dnm1, dnr1))):
        arrived(mains, halo_recv.at[1, i, 0])
        arrived(rims, halo_recv.at[1, i, 1])
    forward_terms((w1m, w1r), (dnm1, dnr1), (upm1, upr1))
    solve(w2m)

    top = LAYERS - 1
    tops = (w2m[at(top), :], rim_x[at(top), :])
    mismatch = [jnp.where(ice[part], tops[part] - seen[part], 0.0) for part in range(2)]
    source = [float(LAYERS) * mismatch[part] for part in range(2)]
    starts = tuple(source[part] * pairs[part][5][at(top), :] for part in range(2))
    adjoints = (am, rim_x)
    for part in range(2):
        adjoints[part][at(top), :] = jnp.where(ice[part], starts[part], 0.0)

    def substitute_first(i, following):
        k = LAYERS - 2 - i
        new = []
        for part in range(2):
            now = -pairs[part][3][at(k), :] * following[part]
            adjoints[part][at(k), :] = jnp.where(ice[part], now, 0.0)
            new.append(now)
        return tuple(new)

    lax.fori_loop(0, LAYERS - 1, substitute_first, starts)
    remote(am, aup, halo_send.at[2, 0, 0], halo_recv.at[2, 0, 0], below)
    remote(am, adn, halo_send.at[2, 1, 0], halo_recv.at[2, 1, 0], above)
    for l in range(SLOTS):
        remote(
            w2m.at[l * 32:l * 32 + 32], vel_in.at[pl.ds(pl.multiple_of(bl * 32, 32), 32)],
            vel_send.at[l], vel_recv.at[bl], holders[l],
        )
    squeeze_rim(ar)

    arrived(aup, halo_recv.at[2, 0, 0])
    arrived(adn, halo_recv.at[2, 1, 0])

    def adjoint_terms(j, carry):
        for c in range(2):
            rows = [load_tiles(am, ar, j, c, r) for r in range(2)]
            for r in range(2):
                right, left = ahead(rows[r]), behind(rows[r])
                for t in range(2):
                    if r == 0:
                        low = adn[pl.ds(j * 64 + (c * 4 + t * 2 + 1), 8, stride=8), :] * has_below
                        high = rows[1][t]
                    else:
                        low = rows[0][t]
                        high = aup[pl.ds(j * 64 + (c * 4 + t * 2), 8, stride=8), :] * has_above
                    east, west, north, south = [faces[j, (r * 2 + t) * 4 + i] for i in range(4)]
                    along = east * high + west * low
                    across = north * right[t] + south * left[t]
                    value = 4.0 * along + across if c == 0 else along + 4.0 * across
                    rhs_m[pl.ds(j * 64 + (c * 4 + t * 2 + r), 8, stride=8), :] = value
        return carry

    lax.fori_loop(0, GROUPS, adjoint_terms, 0)
    zero = jnp.zeros((8, 128), f32)
    rhs_m[at(top), :] = rhs_m[at(top), :] + source[0]

    def eliminate_second(k, prev):
        lower = 1024.0 * (eta_m[at(k - 1), :] + eta_m[at(k), :])
        now = (rhs_m[at(k), :] + lower * prev) * inv_m[at(k), :]
        val_m[at(k), :] = now
        return now

    first = rhs_m[0:8, :] * inv_m[0:8, :]
    val_m[0:8, :] = first
    lax.fori_loop(1, LAYERS, eliminate_second, first)

    def substitute_second(i, following):
        k = LAYERS - 1 - i
        return val_m[at(k), :] - ratio_m[at(k), :] * following

    bottom = jnp.where(ice[0], lax.fori_loop(0, LAYERS, substitute_second, zero), 0.0)

    product = w2m[0:8, :] * bottom
    gradient = -bed[0][0:4, :] * (product[0:4, :] + product[4:8, :])
    grad[...] = gradient
    remote(grad, grad_in, grad_send, grad_recv, (bm, bl))

    lane1 = lax.broadcasted_iota(jnp.int32, (1, 128), 1)
    grad_row = jnp.sum(gradient * gradient, axis=0, keepdims=True)
    fit_row = jnp.sum(0.5 * mismatch[0] * mismatch[0], axis=0, keepdims=True)
    grad_row = grad_row + pltpu.roll(grad_row, 64, 1)
    fit_row = fit_row + pltpu.roll(fit_row, 64, 1)
    row = jnp.where(lane1 < 64, grad_row, fit_row)
    for number, (count, me, peer, row_ref, sum_ref, send_sem, recv_sem) in enumerate(stages):
        row_ref[...] = row
        sum_ref[me] = row
        for i in range(1, count):
            other = lax.rem(me + i, count)
            remote(row_ref, sum_ref.at[me], send_sem.at[i], recv_sem.at[me], peer(other))
        if number == 1:
            for l in range(SLOTS):
                arrived(vel_in.at[l * 32:l * 32 + 32], vel_recv.at[l])
            for c in range(2):
                for kk in range(4):
                    for l in range(SLOTS):
                        to = (c * 4 + kk) * 32 + l * 4
                        vout[to:to + 4, :] = vel_in[l * 32 + kk * 8 + c * 4:l * 32 + kk * 8 + c * 4 + 4, :]
            store = pltpu.make_async_copy(vout, out_hbm, out_sem)
            store.start()
        for i in range(1, count):
            other = lax.rem(me + i, count)
            arrived(sum_ref.at[other], recv_sem.at[other])
        row = sum_ref[0]
        for i in range(1, count):
            row = row + sum_ref[i]

    grad_total = jnp.sum(jnp.where(lane1 < 64, row, 0.0))
    fit_total = jnp.sum(jnp.where(lane1 < 64, 0.0, row))
    misfit_out[0, 0] = fit_total / COLUMNS
    arrived(grad_in, grad_recv)
    scale = jnp.sqrt(jnp.full((4, 128), grad_total, f32) / COLUMNS + 1e-06)
    fric_out[...] = logf[...] - step_size * grad_in[...] / scale

    for copy in sends:
        copy.wait_send()
    for i in range(2):
        for part, src in ((0, w0m), (1, w0r)):
            arrived(src, halo_send.at[0, i, part])
    store.wait()


def on_device(velocity_init, driving, observed, log_friction, ice_mask):
    vel = velocity_init.reshape(2, 4, 2, 16, 128).transpose(0, 1, 3, 2, 4).reshape(256, 128)

    def tiles(a, lead):
        b = a.reshape(lead, 2, 2, 128).transpose(0, 2, 1, 3)
        return b.reshape(lead * 4, 128)

    full, half = (256, 128), (128, 128)
    vm = lambda shape: pltpu.VMEM(shape, f32)
    dma = pltpu.SemaphoreType.DMA
    scratch = [
        vm(full), vm((8, 128)), vm((8, 128)), vm((4, 128)), pltpu.VMEM((4, 128), jnp.int32),
        vm(full), vm(half), vm((24, 128)), vm((3, 24, 128)),
    ]
    scratch += [vm(full), vm(half)] * 3
    scratch += [vm(full), vm(half)] * 4
    scratch += [vm(full), vm(half), vm(full), vm(full)]
    scratch += [vm(full)] * 12 + [vm(full), vm((GROUPS, 16, 8, 128))]
    scratch += [vm(full), vm(full), vm((4, 128)), vm((4, 128))]
    scratch += [vm((1, 128))] * 3 + [vm((8, 1, 128)), vm((8, 1, 128)), vm((16, 1, 128))]
    scratch += [
        dma((5,)), dma, dma((2, 8)), dma((2, 8)), dma((3,)), dma((3,)), dma((3, 2, 2)), dma((3, 2, 2)),
        dma((8,)), dma((8,)), dma, dma,
        dma((8,)), dma((8,)), dma((8,)), dma((8,)), dma((16,)), dma((16,)),
    ]
    anywhere = pl.BlockSpec(memory_space=pl.ANY)
    out, fric, misfit = pl.pallas_call(
        kernel,
        out_shape=(
            jax.ShapeDtypeStruct(full, f32),
            jax.ShapeDtypeStruct((4, 128), f32),
            jax.ShapeDtypeStruct((1, 1), f32),
        ),
        in_specs=[anywhere] * 5,
        out_specs=(
            anywhere,
            pl.BlockSpec(memory_space=pltpu.VMEM),
            pl.BlockSpec(memory_space=pltpu.SMEM),
        ),
        scratch_shapes=scratch,
        compiler_params=pltpu.CompilerParams(collective_id=0, has_side_effects=True),
    )(vel, tiles(driving, 2), tiles(observed, 2), tiles(log_friction, 1), tiles(ice_mask, 1))
    velocity = out.reshape(2, 4, 16, 2, 128).transpose(0, 1, 3, 2, 4).reshape(2, 4, 2, 2048)
    fric = fric.reshape(2, 2, 128).transpose(1, 0, 2).reshape(2, 256)
    return velocity, fric, misfit.reshape(())


def solution(mesh):
    in_specs = (
        P(None, "layer", "map", None),
        P(None, "map", "layer"),
        P(None, "map", "layer"),
        P("map", "layer"),
        P("map", "layer"),
    )
    out_specs = (P(None, "layer", "map", None), P("map", "layer"), P())
    return jax.shard_map(on_device, mesh=mesh, in_specs=in_specs, out_specs=out_specs, check_vma=False)
```

```python
import jax
import jax.numpy as jnp
from jax import lax
from jax.experimental import pallas as pl
from jax.experimental.pallas import tpu as pltpu
from jax.sharding import PartitionSpec as P

strain_floor = 0.1
step_size = 0.5
LAYERS = 32
SLOTS = 8
BLOCKS = 128
GROUPS = 4
COLUMNS = 256 * 2048
MESH = pl.DeviceIdType.MESH
f32 = jnp.float32

SLAB = 40


def place(m):
    return lax.div(m, 8), lax.rem(lax.div(m, 2), 4), lax.rem(m, 2)


def device_at(x, y, z, core):
    return ((z * 4 + lax.rem(y, 4)) * 2 + core, x * 2 + lax.div(y, 4))


def owner_of(m, l):
    z, y_lo, core = place(m)
    y = lax.rem(l, 2) * 4 + y_lo
    odd = lax.rem(z, 2)
    return device_at(lax.div(l, 2), lax.rem(odd * (y + 2) + (1 - odd) * (13 - y), 8), z, core)


def block_of(x, y, z, core):
    odd = lax.rem(z, 2)
    return device_at(x, lax.rem(odd * (y + 6) + (1 - odd) * (13 - y), 8), z, core)


def kernel(
    vel_hbm, drv_hbm, obs_hbm, logf_hbm, mask_hbm,
    out_hbm, fric_out, misfit_out,
    vin, drv, obs, logf, mask, stage, small, small_in,
    w0, w1, w2, dn0, up0, dn1, up1, am, adn, aup, alow, ahigh,
    eta_m, eta_r, diag_m, diag_r, rhs_m, rhs_r, ratio_m, ratio_r, val_m, val_r, inv_m, inv_r, rim_x, faces,
    vel_in, vout, grad, grad_in, row1, row2, sum1, sum2,
    load_sem, out_sem, a2a_send, a2a_recv, small_send, small_recv, halo_send, halo_recv,
    vel_send, vel_recv, grad_send, grad_recv, s1_send, s1_recv, s2_send, s2_recv, token,
):
    M = lax.axis_index("map")
    L = lax.axis_index("layer")
    z, y_lo, core = place(M)
    x = lax.div(L, 2)
    y = lax.rem(L, 2) * 4 + y_lo
    bm, bl = block_of(x, y, z, core)
    below = owner_of(lax.rem(bm + BLOCKS - 1, BLOCKS), bl)
    above = owner_of(lax.rem(bm + 1, BLOCKS), bl)
    owners = [owner_of(M, jnp.int32(l)) for l in range(SLOTS)]
    holders = [(bm, jnp.int32(l)) for l in range(SLOTS)]

    def peer_z(j):
        return device_at(x, y, lax.div(j, 2), lax.rem(j, 2))

    def peer_xy(j):
        return device_at(lax.div(j, 8), lax.rem(j, 8), z, core)

    stages = (
        (z * 2 + core, peer_z, row1, sum1, s1_send, s1_recv),
        (x * 8 + y, peer_xy, row2, sum2, s2_send, s2_recv),
    )

    def along_z(far):
        return device_at(x, y, lax.rem(far, 16), core)

    partners = owners + holders + [below, above, along_z(z + 1), along_z(z + 15)]
    barrier = pltpu.get_barrier_semaphore()
    for partner in partners:
        pl.semaphore_signal(barrier, inc=1, device_id=partner, device_id_type=MESH)

    loads = [
        pltpu.make_async_copy(src, dst, load_sem.at[i])
        for i, (src, dst) in enumerate(
            ((vel_hbm, vin.at[8:264]), (drv_hbm, drv), (obs_hbm, obs), (logf_hbm, logf), (mask_hbm, mask))
        )
    ]
    for load in loads:
        load.start()
    for load in loads[1:]:
        load.wait()
    small[0:8, :] = drv[...]
    small[8:16, :] = obs[...]
    small[16:20, :] = jnp.exp(logf[...]) * (mask[...] == 1).astype(f32)
    small[20:24, :] = (mask[...] != 0).astype(f32)
    loads[0].wait()

    lane2 = lax.broadcasted_iota(jnp.int32, (2, 128), 1)
    lane8 = lax.broadcasted_iota(jnp.int32, (8, 128), 1)
    row8 = lax.broadcasted_iota(jnp.int32, (8, 128), 0)
    zero = jnp.zeros((8, 128), f32)

    def turn(v):
        return pltpu.roll(v, 64, 1)

    def pack(right_a, left_a, right_b, left_b):
        low = jnp.where(lane8 < 32, right_a, turn(left_a))
        return jnp.where(lane8 < 64, low, jnp.where(lane8 < 96, turn(right_b), left_b))

    for c in range(2):
        for kk in range(4):
            for s in range(4):
                stage[pl.ds(kk * 8 + c * 4 + s, 8, stride=SLAB), :] = vin[pl.ds(8 + (c * 4 + kk) * 32 + s, 8, stride=4), :]
        for q in range(2):
            for r in range(2):
                sides = []
                for kk in (2 * q, 2 * q + 1):
                    first = 8 + (c * 4 + kk) * 32 + r
                    sides.append(jnp.where(row8 < SLOTS - 1, vin[pl.ds(first + 4, 8, stride=4), :], 0.0))
                    sides.append(jnp.where(row8 > 0, vin[pl.ds(first - 2, 8, stride=4), :], 0.0))
                stage[pl.ds(32 + q * 4 + c * 2 + r, 8, stride=SLAB), :] = pack(*sides)

    pl.semaphore_wait(barrier, len(partners))

    def give_tokens(level):
        for way, far in ((0, z + (1 << level)), (1, z + 16 - (1 << level))):
            pl.semaphore_signal(token.at[level * 2 + way], inc=1, device_id=along_z(far), device_id_type=MESH)

    def take_tokens(level):
        for way in range(2):
            pl.semaphore_wait(token.at[level * 2 + way], 1)

    give_tokens(0)
    sends = []

    def remote(src, dst, send_sem, recv_sem, device):
        copy = pltpu.make_async_remote_copy(
            src_ref=src, dst_ref=dst, send_sem=send_sem, recv_sem=recv_sem, device_id=device, device_id_type=MESH
        )
        copy.start()
        sends.append(copy)

    def arrived(ref, sem):
        pltpu.make_async_copy(ref, ref, sem).wait()

    rows = pl.ds(pl.multiple_of(L * SLAB, 8), SLAB)
    for l in range(SLOTS):
        remote(stage.at[l * SLAB:l * SLAB + SLAB], w0.at[rows], a2a_send.at[l], a2a_recv.at[L], owners[l])
    for side in range(3):
        target = owner_of(M, lax.rem(L + SLOTS + 1 - side, SLOTS))
        remote(small, small_in.at[side], small_send.at[side], small_recv.at[side], target)

    take_tokens(0)
    give_tokens(1)
    for l in range(SLOTS):
        rows = pl.ds(l * SLAB, SLAB)
        arrived(w0.at[rows], a2a_recv.at[l])
        for i, (device, land) in enumerate(((below, up0), (above, dn0))):
            pltpu.make_async_remote_copy(
                src_ref=w0.at[rows], dst_ref=land.at[rows], send_sem=halo_send.at[0, i],
                recv_sem=halo_recv.at[0, i], device_id=device, device_id_type=MESH,
            ).start()

    take_tokens(1)
    give_tokens(2)
    for side in range(3):
        arrived(small_in.at[side], small_recv.at[side])
    has_left = (bl > 0).astype(f32)
    has_right = (bl < SLOTS - 1).astype(f32)
    has_below = (bm > 0).astype(f32)
    has_above = (bm < BLOCKS - 1).astype(f32)

    def double(rows):
        return jnp.concatenate([rows, rows], 0)

    def rim_rows(start, comps):
        parts = []
        for c in range(comps):
            at = start + 4 * c
            parts.append(jnp.where(lane2 < 64, small_in[2, at:at + 2, :] * has_right, small_in[0, at + 2:at + 4, :] * has_left))
        if comps == 1:
            parts = parts * 2
        return double(jnp.concatenate(parts, 0))

    drive = (small_in[1, 0:8, :], rim_rows(0, 2))
    seen = (small_in[1, 8:16, :], rim_rows(8, 2))
    bed = (double(small_in[1, 16:20, :]), rim_rows(16, 1))
    ice = (double(small_in[1, 20:24, :]) > 0.5, rim_rows(20, 1) > 0.5)

    def ahead(tiles):
        turned = [pltpu.roll(t, 127, 1) for t in tiles]
        return [jnp.where(lane8 == 127, turned[(i + 1) % 3], turned[i]) for i in range(3)]

    def behind(tiles):
        turned = [pltpu.roll(t, 1, 1) for t in tiles]
        return [jnp.where(lane8 == 0, turned[(i + 2) % 3], turned[i]) for i in range(3)]

    def load_tiles(slab, c, r, kk, packed):
        tiles = [slab[pl.ds(kk * 8 + c * 4 + t * 2 + r, 8, stride=SLAB), :] for t in range(2)]
        return tiles + [packed[kk % 2]]

    def unpack(slab, c, r, q):
        v = slab[pl.ds(32 + q * 4 + c * 2 + r, 8, stride=SLAB), :]
        turned = turn(v)
        return jnp.where(lane8 < 64, v, turned), jnp.where(lane8 < 64, turned, v)

    def store_tile(main, rim, kk, c, t, r, value):
        if t < 2:
            main[pl.ds(kk * 8 + c * 4 + t * 2 + r, 8, stride=32), :] = value
        else:
            rim[pl.ds(kk * 8 + c * 2 + r, 8, stride=32), :] = value

    def scaled(tiles, factor):
        return [t * factor for t in tiles]

    def forward_terms(own, low, high):
        for q in range(2):
            rims = [[unpack(slab, c, r, q) for slab in (low, own, high) for r in range(2)] for c in range(2)]
            for kk in (2 * q, 2 * q + 1):
                group(own, low, high, kk, rims)

    def group(own, low, high, kk, rims):
        w = []
        for c in range(2):
            rows = [scaled(load_tiles(low, c, r, kk, rims[c][r]), has_below) for r in range(2)]
            rows += [load_tiles(own, c, r, kk, rims[c][2 + r]) for r in range(2)]
            rows += [scaled(load_tiles(high, c, r, kk, rims[c][4 + r]), has_above) for r in range(2)]
            w.append(rows)
        right = [[ahead(w[c][r]) for r in range(1, 5)] for c in range(2)]
        left = [[behind(w[c][r]) for r in range(1, 5)] for c in range(2)]
        eta = []
        for r in range(4):
            tiles = []
            for t in range(3):
                u_x = (w[0][r + 2][t] - w[0][r][t]) * 0.5
                v_x = (w[1][r + 2][t] - w[1][r][t]) * 0.5
                u_y = (right[0][r][t] - left[0][r][t]) * 0.5
                v_y = (right[1][r][t] - left[1][r][t]) * 0.5
                shear = u_y + v_x
                rate = u_x * u_x + v_y * v_y + u_x * v_y + 0.25 * shear * shear
                tiles.append(jnp.exp(jnp.log(strain_floor + rate) * (-1.0 / 3.0)))
            eta.append(tiles)
        for r in range(2):
            eta_right, eta_left = ahead(eta[r + 1]), behind(eta[r + 1])
            for t in range(3):
                centre = eta[r + 1][t]
                east = 0.5 * (centre + eta[r + 2][t])
                west = 0.5 * (centre + eta[r][t])
                north = 0.5 * (centre + eta_right[t])
                south = 0.5 * (centre + eta_left[t])
                along, across = east + west, north + south
                if t < 2:
                    for i, face in enumerate((east, west, north, south)):
                        faces[kk, (r * 2 + t) * 4 + i] = face
                u, v = w
                sum_u = (
                    4.0 * (east * u[r + 3][t] + west * u[r + 1][t])
                    + north * right[0][r + 1][t] + south * left[0][r + 1][t]
                )
                sum_v = (
                    east * v[r + 3][t] + west * v[r + 1][t]
                    + 4.0 * (north * right[1][r + 1][t] + south * left[1][r + 1][t])
                )
                store_tile(eta_m, eta_r, kk, 0, t, r, centre)
                store_tile(eta_m, eta_r, kk, 1, t, r, centre)
                store_tile(diag_m, diag_r, kk, 0, t, r, 4.0 * along + across)
                store_tile(diag_m, diag_r, kk, 1, t, r, along + 4.0 * across)
                store_tile(rhs_m, rhs_r, kk, 0, t, r, sum_u)
                store_tile(rhs_m, rhs_r, kk, 1, t, r, sum_v)

    pairs = (
        (eta_m, diag_m, rhs_m, ratio_m, val_m, inv_m),
        (eta_r, diag_r, rhs_r, ratio_r, val_r, inv_r),
    )

    def at(k):
        return pl.ds(pl.multiple_of(k * 8, 8), 8)

    def solve(out):
        def eliminate(k, carry, last=False):
            new = []
            for part in range(2):
                eta, diag, rhs, ratio, val, inv = pairs[part]
                lower, ratio_prev, val_prev, pad = carry[part]
                upper = zero if last else 1024.0 * (eta[at(k), :] + eta[at(k + 1), :])
                inverse = 1.0 / (((lower + upper + pad) + diag[at(k), :]) + lower * ratio_prev)
                ratio_now = -upper * inverse
                val_now = (drive[part] + rhs[at(k), :] + lower * val_prev) * inverse
                ratio[at(k), :] = ratio_now
                val[at(k), :] = val_now
                inv[at(k), :] = inverse
                new.append((upper, ratio_now, val_now, zero))
            return tuple(new)

        carry = tuple((zero, zero, zero, bed[part]) for part in range(2))
        carry = lax.fori_loop(0, LAYERS - 1, eliminate, carry)
        eliminate(LAYERS - 1, carry, last=True)

        def substitute(i, following):
            slot = SLOTS - 1 - i
            for kk in reversed(range(4)):
                k = slot * 4 + kk
                new = []
                for part, (to, where) in enumerate(((out, pl.ds(pl.multiple_of(slot * SLAB + kk * 8, 8), 8)), (rim_x, at(k)))):
                    ratio, val = pairs[part][3], pairs[part][4]
                    now = val[at(k), :] - ratio[at(k), :] * following[part]
                    to[where, :] = jnp.where(ice[part], now, 0.0)
                    new.append(now)
                following = tuple(new)
            return following

        lax.fori_loop(0, SLOTS, substitute, (zero, zero))

    def pack_rims(out):
        for q in range(2):
            for s in range(4):
                a = rim_x[pl.ds(2 * q * 8 + s, 8, stride=32), :]
                b = rim_x[pl.ds((2 * q + 1) * 8 + s, 8, stride=32), :]
                out[pl.ds(32 + q * 4 + s, 8, stride=SLAB), :] = pack(a, a, b, b)

    for i, land in enumerate((up0, dn0)):
        arrived(land, halo_recv.at[0, i])
    forward_terms(w0, dn0, up0)
    solve(w1)
    pack_rims(w1)
    for i, (device, land) in enumerate(((below, up1), (above, dn1))):
        remote(w1, land, halo_send.at[1, i], halo_recv.at[1, i], device)

    for i, land in enumerate((up1, dn1)):
        arrived(land, halo_recv.at[1, i])
    forward_terms(w1, dn1, up1)
    solve(w2)
    take_tokens(2)

    top = LAYERS - 1
    last = (SLOTS - 1) * SLAB + 24
    tops = (w2[last:last + 8, :], rim_x[at(top), :])
    mismatch = [jnp.where(ice[part], tops[part] - seen[part], 0.0) for part in range(2)]
    source = [float(LAYERS) * mismatch[part] for part in range(2)]
    starts = tuple(source[part] * pairs[part][5][at(top), :] for part in range(2))
    adjoints = (am, rim_x)
    for part in range(2):
        adjoints[part][at(top), :] = jnp.where(ice[part], starts[part], 0.0)

    def substitute_first(i, following):
        k = LAYERS - 2 - i
        new = []
        for part in range(2):
            now = -pairs[part][3][at(k), :] * following[part]
            adjoints[part][at(k), :] = jnp.where(ice[part], now, 0.0)
            new.append(now)
        return tuple(new)

    lax.fori_loop(0, LAYERS - 1, substitute_first, starts)
    for r, (edge, land, device) in enumerate(((alow, aup, below), (ahigh, adn, above))):
        for s in range(4):
            for j in range(GROUPS):
                edge[pl.ds(j * 4 + s, 8, stride=16), :] = am[pl.ds(j * 8 + s * 2 + r, 8, stride=32), :]
        remote(edge, land, halo_send.at[2, r], halo_recv.at[2, r], device)

    arrived(aup, halo_recv.at[2, 0])
    arrived(adn, halo_recv.at[2, 1])

    for kk in range(4):
        for c in range(2):
            rows = [[am[pl.ds(kk * 8 + c * 4 + t * 2 + r, 8, stride=32), :] for t in range(2)] for r in range(2)]
            for r in range(2):
                rows[r].append(rim_x[pl.ds(kk * 8 + c * 2 + r, 8, stride=32), :])
            for r in range(2):
                right, left = ahead(rows[r]), behind(rows[r])
                for t in range(2):
                    if r == 0:
                        low = adn[pl.ds(kk * 4 + c * 2 + t, 8, stride=16), :] * has_below
                        high = rows[1][t]
                    else:
                        low = rows[0][t]
                        high = aup[pl.ds(kk * 4 + c * 2 + t, 8, stride=16), :] * has_above
                    east, west, north, south = [faces[kk, (r * 2 + t) * 4 + i] for i in range(4)]
                    along = east * high + west * low
                    across = north * right[t] + south * left[t]
                    value = 4.0 * along + across if c == 0 else along + 4.0 * across
                    rhs_m[pl.ds(kk * 8 + c * 4 + t * 2 + r, 8, stride=32), :] = value
    rhs_m[at(top), :] = rhs_m[at(top), :] + source[0]

    def eliminate_second(k, prev):
        lower = 1024.0 * (eta_m[at(k - 1), :] + eta_m[at(k), :])
        now = (rhs_m[at(k), :] + lower * prev) * inv_m[at(k), :]
        val_m[at(k), :] = now
        return now

    first = rhs_m[0:8, :] * inv_m[0:8, :]
    val_m[0:8, :] = first
    lax.fori_loop(1, LAYERS, eliminate_second, first)

    def substitute_second(i, following):
        k = LAYERS - 1 - i
        return val_m[at(k), :] - ratio_m[at(k), :] * following

    bottom = jnp.where(ice[0], lax.fori_loop(0, LAYERS, substitute_second, zero), 0.0)

    product = w2[0:8, :] * bottom
    gradient = -bed[0][0:4, :] * (product[0:4, :] + product[4:8, :])
    grad[...] = gradient
    remote(grad, grad_in, grad_send, grad_recv, (bm, bl))

    lane1 = lax.broadcasted_iota(jnp.int32, (1, 128), 1)
    grad_row = jnp.sum(gradient * gradient, axis=0, keepdims=True)
    fit_row = jnp.sum(0.5 * mismatch[0] * mismatch[0], axis=0, keepdims=True)
    grad_row = grad_row + pltpu.roll(grad_row, 64, 1)
    fit_row = fit_row + pltpu.roll(fit_row, 64, 1)
    row = jnp.where(lane1 < 64, grad_row, fit_row)
    for number, (me, peer, row_ref, sum_ref, send_sem, recv_sem) in enumerate(stages):
        count = 32
        row_ref[...] = row
        sum_ref[me] = row
        order = sorted(range(1, count), key=lambda i: -min(i, count - i)) if number == 0 else reversed(range(1, count))
        for i in order:
            other = lax.rem(me + i, count)
            remote(row_ref, sum_ref.at[me], send_sem.at[i], recv_sem.at[me], peer(other))
        if number == 0:
            for l in range(SLOTS):
                remote(
                    w2.at[l * SLAB:l * SLAB + 32], vel_in.at[pl.ds(pl.multiple_of(bl * 32, 32), 32)],
                    vel_send.at[l], vel_recv.at[bl], holders[l],
                )
        else:
            for l in range(SLOTS):
                arrived(vel_in.at[l * 32:l * 32 + 32], vel_recv.at[l])
            for c in range(2):
                for kk in range(4):
                    for s in range(4):
                        piece = vel_in[pl.ds(kk * 8 + c * 4 + s, 8, stride=32), :]
                        vout[pl.ds((c * 4 + kk) * 32 + s, 8, stride=4), :] = piece
            store = pltpu.make_async_copy(vout, out_hbm, out_sem)
            store.start()
        for i in range(1, count):
            other = lax.rem(me + i, count)
            arrived(sum_ref.at[other], recv_sem.at[other])
        parts = [sum_ref[i] for i in range(count)]
        while len(parts) > 1:
            parts = [parts[i] + parts[i + 1] for i in range(0, len(parts), 2)]
        row = parts[0]

    grad_total = jnp.sum(jnp.where(lane1 < 64, row, 0.0))
    fit_total = jnp.sum(jnp.where(lane1 < 64, 0.0, row))
    misfit_out[0, 0] = fit_total / COLUMNS
    arrived(grad_in, grad_recv)
    scale = jnp.sqrt(jnp.full((4, 128), grad_total, f32) / COLUMNS + 1e-06)
    fric_out[...] = logf[...] - step_size * grad_in[...] / scale

    for copy in sends:
        copy.wait_send()
    for i in range(2):
        arrived(w0, halo_send.at[0, i])
    store.wait()


def on_device(velocity_init, driving, observed, log_friction, ice_mask):
    vel = velocity_init.reshape(2, 4, 2, 16, 128).transpose(0, 1, 3, 2, 4).reshape(256, 128)

    def tiles(a, lead):
        b = a.reshape(lead, 2, 2, 128).transpose(0, 2, 1, 3)
        return b.reshape(lead * 4, 128)

    full, half, slab = (256, 128), (128, 128), (SLOTS * SLAB, 128)
    vm = lambda shape: pltpu.VMEM(shape, f32)
    dma = pltpu.SemaphoreType.DMA
    scratch = [vm((272, 128)), vm((8, 128)), vm((8, 128)), vm((4, 128)), pltpu.VMEM((4, 128), jnp.int32)]
    scratch += [vm(slab), vm((24, 128)), vm((3, 24, 128))]
    scratch += [vm(slab)] * 7 + [vm(full)] + [vm(half)] * 4
    scratch += [vm(full)] * 13 + [vm((GROUPS, 16, 8, 128))]
    scratch += [vm(full), vm(full), vm((4, 128)), vm((4, 128))]
    scratch += [vm((1, 128))] * 2 + [vm((32, 1, 128))] * 2
    scratch += [dma((5,)), dma, dma((8,)), dma((8,)), dma((3,)), dma((3,)), dma((3, 2)), dma((3, 2))]
    scratch += [dma((8,)), dma((8,)), dma, dma] + [dma((32,))] * 4 + [pltpu.SemaphoreType.REGULAR((6,))]
    anywhere = pl.BlockSpec(memory_space=pl.ANY)
    out, fric, misfit = pl.pallas_call(
        kernel,
        out_shape=(
            jax.ShapeDtypeStruct(full, f32),
            jax.ShapeDtypeStruct((4, 128), f32),
            jax.ShapeDtypeStruct((1, 1), f32),
        ),
        in_specs=[anywhere] * 5,
        out_specs=(
            anywhere,
            pl.BlockSpec(memory_space=pltpu.VMEM),
            pl.BlockSpec(memory_space=pltpu.SMEM),
        ),
        scratch_shapes=scratch,
        compiler_params=pltpu.CompilerParams(collective_id=0, has_side_effects=True),
    )(vel, tiles(driving, 2), tiles(observed, 2), tiles(log_friction, 1), tiles(ice_mask, 1))
    velocity = out.reshape(2, 4, 16, 2, 128).transpose(0, 1, 3, 2, 4).reshape(2, 4, 2, 2048)
    fric = fric.reshape(2, 2, 128).transpose(1, 0, 2).reshape(2, 256)
    return velocity, fric, misfit.reshape(())


def solution(mesh):
    in_specs = (
        P(None, "layer", "map", None),
        P(None, "map", "layer"),
        P(None, "map", "layer"),
        P("map", "layer"),
        P("map", "layer"),
    )
    out_specs = (P(None, "layer", "map", None), P("map", "layer"), P())
    return jax.shard_map(on_device, mesh=mesh, in_specs=in_specs, out_specs=out_specs, check_vma=False)
```

```python
import jax
import jax.numpy as jnp
from jax import lax
from jax.experimental import pallas as pl
from jax.experimental.pallas import tpu as pltpu
from jax.sharding import PartitionSpec as P

strain_floor = 0.1
step_size = 0.5
LAYERS = 32
SLOTS = 8
BLOCKS = 128
GROUPS = 4
COLUMNS = 256 * 2048
MESH = pl.DeviceIdType.MESH
f32 = jnp.float32

SLAB = 40


def place(m):
    return lax.div(m, 8), lax.rem(lax.div(m, 2), 4), lax.rem(m, 2)


def device_at(x, y, z, core):
    return ((z * 4 + lax.rem(y, 4)) * 2 + core, x * 2 + lax.div(y, 4))


def owner_of(m, l):
    z, y_lo, core = place(m)
    y = lax.rem(l, 2) * 4 + y_lo
    odd = lax.rem(z, 2)
    return device_at(lax.div(l, 2), lax.rem(odd * (y + 2) + (1 - odd) * (13 - y), 8), z, core)


def block_of(x, y, z, core):
    odd = lax.rem(z, 2)
    return device_at(x, lax.rem(odd * (y + 6) + (1 - odd) * (13 - y), 8), z, core)


def kernel(
    vel_hbm, drv_hbm, obs_hbm, logf_hbm, mask_hbm,
    vout, fric_out, misfit_out,
    vin, drv, obs, logf, mask, stage, small, small_in,
    w0, w1, w2, dn0, up0, dn1, up1, am, adn, aup, alow, ahigh,
    eta_m, eta_r, diag_m, diag_r, rhs_m, rhs_r, ratio_m, ratio_r, val_m, val_r, inv_m, inv_r, rim_x, faces,
    vel_in, grad, grad_in, row1, row2, sum1, sum2,
    load_sem, a2a_send, a2a_recv, small_send, small_recv, halo_send, halo_recv,
    vel_send, vel_recv, grad_send, grad_recv, s1_send, s1_recv, s2_send, s2_recv, token,
):
    loads = [
        pltpu.make_async_copy(src, dst, load_sem.at[i])
        for i, (src, dst) in enumerate(
            ((vel_hbm, vin.at[8:264]), (drv_hbm, drv), (obs_hbm, obs), (logf_hbm, logf), (mask_hbm, mask))
        )
    ]
    for load in loads:
        load.start()

    M = lax.axis_index("map")
    L = lax.axis_index("layer")
    z, y_lo, core = place(M)
    x = lax.div(L, 2)
    y = lax.rem(L, 2) * 4 + y_lo
    bm, bl = block_of(x, y, z, core)
    below = owner_of(lax.rem(bm + BLOCKS - 1, BLOCKS), bl)
    above = owner_of(lax.rem(bm + 1, BLOCKS), bl)
    owners = [owner_of(M, jnp.int32(l)) for l in range(SLOTS)]
    holders = [(bm, jnp.int32(l)) for l in range(SLOTS)]

    def peer_z(j):
        return device_at(x, y, lax.div(j, 2), lax.rem(j, 2))

    def peer_xy(j):
        return device_at(lax.div(j, 8), lax.rem(j, 8), z, core)

    ring_z = sorted(((dz, dc) for dz in range(16) for dc in range(2)), key=lambda d: -min(d[0], 16 - d[0]) - d[1] / 2)[:-1]
    ring_xy = sorted(((dx, dy) for dx in range(4) for dy in range(8)), key=lambda d: -min(d[0], 4 - d[0]) - min(d[1], 8 - d[1]))[:-1]
    zs = [lax.rem(z + dz, 16) for dz in range(16)]
    xs = [lax.rem(x + dx, 4) for dx in range(4)]
    ys = [lax.rem(y + dy, 8) for dy in range(8)]
    stages = (
        (z * 2 + core, [zs[dz] * 2 + (1 - core if dc else core) for dz, dc in ring_z], peer_z, row1, sum1, s1_send, s1_recv),
        (x * 8 + y, [xs[dx] * 8 + ys[dy] for dx, dy in ring_xy], peer_xy, row2, sum2, s2_send, s2_recv),
    )

    def along_z(far):
        return device_at(x, y, lax.rem(far, 16), core)

    partners = owners + holders + [below, above, along_z(z + 1), along_z(z + 15)]
    barrier = pltpu.get_barrier_semaphore()
    for partner in partners:
        pl.semaphore_signal(barrier, inc=1, device_id=partner, device_id_type=MESH)

    for load in loads[1:]:
        load.wait()
    small[0:8, :] = drv[...]
    small[8:16, :] = obs[...]
    small[16:20, :] = jnp.exp(logf[...]) * (mask[...] == 1).astype(f32)
    small[20:24, :] = (mask[...] != 0).astype(f32)
    loads[0].wait()

    lane2 = lax.broadcasted_iota(jnp.int32, (2, 128), 1)
    lane8 = lax.broadcasted_iota(jnp.int32, (8, 128), 1)
    row8 = lax.broadcasted_iota(jnp.int32, (8, 128), 0)
    zero = jnp.zeros((8, 128), f32)

    def turn(v):
        return pltpu.roll(v, 64, 1)

    def pack(right_a, left_a, right_b, left_b):
        low = jnp.where(lane8 < 32, right_a, turn(left_a))
        return jnp.where(lane8 < 64, low, jnp.where(lane8 < 96, turn(right_b), left_b))

    for c in range(2):
        for kk in range(4):
            for s in range(4):
                stage[pl.ds(kk * 8 + c * 4 + s, 8, stride=SLAB), :] = vin[pl.ds(8 + (c * 4 + kk) * 32 + s, 8, stride=4), :]
        for q in range(2):
            for r in range(2):
                sides = []
                for kk in (2 * q, 2 * q + 1):
                    first = 8 + (c * 4 + kk) * 32 + r
                    sides.append(jnp.where(row8 < SLOTS - 1, vin[pl.ds(first + 4, 8, stride=4), :], 0.0))
                    sides.append(jnp.where(row8 > 0, vin[pl.ds(first - 2, 8, stride=4), :], 0.0))
                stage[pl.ds(32 + q * 4 + c * 2 + r, 8, stride=SLAB), :] = pack(*sides)

    pl.semaphore_wait(barrier, len(partners))

    def give_tokens(level):
        for way, far in ((0, z + (1 << level)), (1, z + 16 - (1 << level))):
            pl.semaphore_signal(token.at[level * 2 + way], inc=1, device_id=along_z(far), device_id_type=MESH)

    def take_tokens(level):
        for way in range(2):
            pl.semaphore_wait(token.at[level * 2 + way], 1)

    give_tokens(0)
    sends = []

    def remote(src, dst, send_sem, recv_sem, device):
        copy = pltpu.make_async_remote_copy(
            src_ref=src, dst_ref=dst, send_sem=send_sem, recv_sem=recv_sem, device_id=device, device_id_type=MESH
        )
        copy.start()
        sends.append(copy)

    bulk = []

    def pieces(src, dst, count, index, device):
        size = src.shape[0] // count
        for i in reversed(range(count)):
            rows = pl.ds(i * size, size)
            pltpu.make_async_remote_copy(
                src_ref=src.at[rows], dst_ref=dst.at[rows], send_sem=halo_send.at[index],
                recv_sem=halo_recv.at[index], device_id=device, device_id_type=MESH,
            ).start()
        bulk.append((src, halo_send.at[index]))

    def arrived(ref, sem):
        pltpu.make_async_copy(ref, ref, sem).wait()

    rows = pl.ds(pl.multiple_of(L * SLAB, 8), SLAB)
    for l in range(SLOTS):
        remote(stage.at[l * SLAB:l * SLAB + SLAB], w0.at[rows], a2a_send.at[l], a2a_recv.at[L], owners[l])
    for side in range(3):
        target = owner_of(M, lax.rem(L + SLOTS + 1 - side, SLOTS))
        remote(small, small_in.at[side], small_send.at[side], small_recv.at[side], target)

    take_tokens(0)
    give_tokens(1)
    for l in range(SLOTS):
        rows = pl.ds(l * SLAB, SLAB)
        arrived(w0.at[rows], a2a_recv.at[l])
        for i, (device, land) in enumerate(((below, up0), (above, dn0))):
            pltpu.make_async_remote_copy(
                src_ref=w0.at[rows], dst_ref=land.at[rows], send_sem=halo_send.at[0, i],
                recv_sem=halo_recv.at[0, i], device_id=device, device_id_type=MESH,
            ).start()

    take_tokens(1)
    give_tokens(2)
    for side in range(3):
        arrived(small_in.at[side], small_recv.at[side])
    has_left = (bl > 0).astype(f32)
    has_right = (bl < SLOTS - 1).astype(f32)
    has_below = (bm > 0).astype(f32)
    has_above = (bm < BLOCKS - 1).astype(f32)

    def double(rows):
        return jnp.concatenate([rows, rows], 0)

    def rim_rows(start, comps):
        parts = []
        for c in range(comps):
            at = start + 4 * c
            parts.append(jnp.where(lane2 < 64, small_in[2, at:at + 2, :] * has_right, small_in[0, at + 2:at + 4, :] * has_left))
        if comps == 1:
            parts = parts * 2
        return double(jnp.concatenate(parts, 0))

    drive = (small_in[1, 0:8, :], rim_rows(0, 2))
    seen = (small_in[1, 8:16, :], rim_rows(8, 2))
    bed = (double(small_in[1, 16:20, :]), rim_rows(16, 1))
    ice = (double(small_in[1, 20:24, :]) > 0.5, rim_rows(20, 1) > 0.5)

    def ahead(tiles):
        turned = [pltpu.roll(t, 127, 1) for t in tiles]
        return [jnp.where(lane8 == 127, turned[(i + 1) % 3], turned[i]) for i in range(3)]

    def behind(tiles):
        turned = [pltpu.roll(t, 1, 1) for t in tiles]
        return [jnp.where(lane8 == 0, turned[(i + 2) % 3], turned[i]) for i in range(3)]

    def load_tiles(slab, c, r, kk, packed):
        tiles = [slab[pl.ds(kk * 8 + c * 4 + t * 2 + r, 8, stride=SLAB), :] for t in range(2)]
        return tiles + [packed[kk % 2]]

    def unpack(slab, c, r, q):
        v = slab[pl.ds(32 + q * 4 + c * 2 + r, 8, stride=SLAB), :]
        turned = turn(v)
        return jnp.where(lane8 < 64, v, turned), jnp.where(lane8 < 64, turned, v)

    def store_tile(main, rim, kk, c, t, r, value):
        if t < 2:
            main[pl.ds(kk * 8 + c * 4 + t * 2 + r, 8, stride=SLAB), :] = value
        else:
            rim[pl.ds(kk * 8 + c * 2 + r, 8, stride=SLAB), :] = value

    def scaled(tiles, factor):
        return [t * factor for t in tiles]

    def forward_terms(own, low, high):
        for q in range(2):
            rims = [[unpack(slab, c, r, q) for slab in (low, own, high) for r in range(2)] for c in range(2)]
            for kk in (2 * q, 2 * q + 1):
                group(own, low, high, kk, rims)

    def group(own, low, high, kk, rims):
        w = []
        for c in range(2):
            rows = [scaled(load_tiles(low, c, r, kk, rims[c][r]), has_below) for r in range(2)]
            rows += [load_tiles(own, c, r, kk, rims[c][2 + r]) for r in range(2)]
            rows += [scaled(load_tiles(high, c, r, kk, rims[c][4 + r]), has_above) for r in range(2)]
            w.append(rows)
        right = [[ahead(w[c][r]) for r in range(1, 5)] for c in range(2)]
        left = [[behind(w[c][r]) for r in range(1, 5)] for c in range(2)]
        eta = []
        for r in range(4):
            tiles = []
            for t in range(3):
                u_x = (w[0][r + 2][t] - w[0][r][t]) * 0.5
                v_x = (w[1][r + 2][t] - w[1][r][t]) * 0.5
                u_y = (right[0][r][t] - left[0][r][t]) * 0.5
                v_y = (right[1][r][t] - left[1][r][t]) * 0.5
                shear = u_y + v_x
                rate = u_x * u_x + v_y * v_y + u_x * v_y + 0.25 * shear * shear
                tiles.append(jnp.exp(jnp.log(strain_floor + rate) * (-1.0 / 3.0)))
            eta.append(tiles)
        for r in range(2):
            eta_right, eta_left = ahead(eta[r + 1]), behind(eta[r + 1])
            for t in range(3):
                centre = eta[r + 1][t]
                east = 0.5 * (centre + eta[r + 2][t])
                west = 0.5 * (centre + eta[r][t])
                north = 0.5 * (centre + eta_right[t])
                south = 0.5 * (centre + eta_left[t])
                along, across = east + west, north + south
                if t < 2:
                    for i, face in enumerate((east, west, north, south)):
                        faces[kk, (r * 2 + t) * 4 + i] = face
                u, v = w
                sum_u = (
                    4.0 * (east * u[r + 3][t] + west * u[r + 1][t])
                    + north * right[0][r + 1][t] + south * left[0][r + 1][t]
                )
                sum_v = (
                    east * v[r + 3][t] + west * v[r + 1][t]
                    + 4.0 * (north * right[1][r + 1][t] + south * left[1][r + 1][t])
                )
                store_tile(eta_m, eta_r, kk, 0, t, r, centre)
                store_tile(eta_m, eta_r, kk, 1, t, r, centre)
                store_tile(diag_m, diag_r, kk, 0, t, r, 4.0 * along + across)
                store_tile(diag_m, diag_r, kk, 1, t, r, along + 4.0 * across)
                store_tile(rhs_m, rhs_r, kk, 0, t, r, sum_u)
                store_tile(rhs_m, rhs_r, kk, 1, t, r, sum_v)

    pairs = (
        (eta_m, diag_m, rhs_m, ratio_m, val_m, inv_m),
        (eta_r, diag_r, rhs_r, ratio_r, val_r, inv_r),
    )

    def at(slot, kk):
        return pl.ds(pl.multiple_of(slot * SLAB + kk * 8, 8), 8)

    def solve(out):
        def eliminate(slot, carry, last=False):
            for kk in range(4):
                new = []
                for part in range(2):
                    eta, diag, rhs, ratio, val, inv = pairs[part]
                    lower, ratio_prev, val_prev, pad = carry[part]
                    k = at(slot, kk)
                    if last and kk == 3:
                        upper = zero
                    else:
                        upper = 1024.0 * (eta[k, :] + eta[at(slot, kk + 1) if kk < 3 else at(slot + 1, 0), :])
                    inverse = 1.0 / (((lower + upper + pad) + diag[k, :]) + lower * ratio_prev)
                    ratio_now = -upper * inverse
                    val_now = (drive[part] + rhs[k, :] + lower * val_prev) * inverse
                    ratio[k, :] = ratio_now
                    val[k, :] = val_now
                    inv[k, :] = inverse
                    new.append((upper, ratio_now, val_now, zero))
                carry = tuple(new)
            return carry

        carry = tuple((zero, zero, zero, bed[part]) for part in range(2))
        carry = lax.fori_loop(0, SLOTS - 1, eliminate, carry)
        eliminate(SLOTS - 1, carry, last=True)

        def substitute(i, following):
            slot = SLOTS - 1 - i
            for kk in reversed(range(4)):
                k = at(slot, kk)
                new = []
                for part, to in enumerate((out, rim_x)):
                    ratio, val = pairs[part][3], pairs[part][4]
                    now = val[k, :] - ratio[k, :] * following[part]
                    to[k, :] = jnp.where(ice[part], now, 0.0)
                    new.append(now)
                following = tuple(new)
            return following

        lax.fori_loop(0, SLOTS, substitute, (zero, zero))

    def pack_rims(out):
        for q in range(2):
            for s in range(4):
                a = rim_x[pl.ds(2 * q * 8 + s, 8, stride=SLAB), :]
                b = rim_x[pl.ds((2 * q + 1) * 8 + s, 8, stride=SLAB), :]
                out[pl.ds(32 + q * 4 + s, 8, stride=SLAB), :] = pack(a, a, b, b)

    for i, land in enumerate((up0, dn0)):
        arrived(land, halo_recv.at[0, i])
    forward_terms(w0, dn0, up0)
    solve(w1)
    pack_rims(w1)
    for i, (device, land) in enumerate(((below, up1), (above, dn1))):
        pieces(w1, land, SLOTS, (1, i), device)

    for i, land in enumerate((up1, dn1)):
        arrived(land, halo_recv.at[1, i])
    forward_terms(w1, dn1, up1)
    solve(w2)
    take_tokens(2)

    top = pl.ds((SLOTS - 1) * SLAB + 24, 8)
    tops = (w2[top, :], rim_x[top, :])
    mismatch = [jnp.where(ice[part], tops[part] - seen[part], 0.0) for part in range(2)]
    source = [float(LAYERS) * mismatch[part] for part in range(2)]
    starts = tuple(source[part] * pairs[part][5][top, :] for part in range(2))
    adjoints = (am, rim_x)
    for part in range(2):
        adjoints[part][top, :] = jnp.where(ice[part], starts[part], 0.0)

    def substitute_first(slot, following, steps=range(4)):
        for kk in reversed(steps):
            k = at(slot, kk)
            new = []
            for part in range(2):
                now = -pairs[part][3][k, :] * following[part]
                adjoints[part][k, :] = jnp.where(ice[part], now, 0.0)
                new.append(now)
            following = tuple(new)
        return following

    following = substitute_first(SLOTS - 1, starts, range(3))
    lax.fori_loop(1, SLOTS, lambda i, carry: substitute_first(SLOTS - 1 - i, carry), following)
    for r, (edge, land, device) in enumerate(((alow, aup, below), (ahigh, adn, above))):
        for s in range(4):
            for j in range(GROUPS):
                edge[pl.ds(j * 32 + s, 8, stride=4), :] = am[pl.ds(j * 8 + s * 2 + r, 8, stride=SLAB), :]
        pieces(edge, land, 4, (2, r), device)

    arrived(aup, halo_recv.at[2, 0])
    arrived(adn, halo_recv.at[2, 1])

    for kk in range(4):
        for c in range(2):
            rows = [[am[pl.ds(kk * 8 + c * 4 + t * 2 + r, 8, stride=SLAB), :] for t in range(2)] for r in range(2)]
            for r in range(2):
                rows[r].append(rim_x[pl.ds(kk * 8 + c * 2 + r, 8, stride=SLAB), :])
            for r in range(2):
                right, left = ahead(rows[r]), behind(rows[r])
                for t in range(2):
                    if r == 0:
                        low = adn[pl.ds(kk * 32 + c * 2 + t, 8, stride=4), :] * has_below
                        high = rows[1][t]
                    else:
                        low = rows[0][t]
                        high = aup[pl.ds(kk * 32 + c * 2 + t, 8, stride=4), :] * has_above
                    east, west, north, south = [faces[kk, (r * 2 + t) * 4 + i] for i in range(4)]
                    along = east * high + west * low
                    across = north * right[t] + south * left[t]
                    value = 4.0 * along + across if c == 0 else along + 4.0 * across
                    rhs_m[pl.ds(kk * 8 + c * 4 + t * 2 + r, 8, stride=SLAB), :] = value
    rhs_m[top, :] = rhs_m[top, :] + source[0]

    def eliminate_second(slot, prev, steps=range(4)):
        for kk in steps:
            k, under = at(slot, kk), at(slot, kk - 1) if kk > 0 else at(slot - 1, 3)
            lower = 1024.0 * (eta_m[under, :] + eta_m[k, :])
            inverse = inv_m[k, :]
            prev = rhs_m[k, :] * inverse + (lower * inverse) * prev
            val_m[k, :] = prev
        return prev

    first = rhs_m[0:8, :] * inv_m[0:8, :]
    val_m[0:8, :] = first
    lax.fori_loop(1, SLOTS, eliminate_second, eliminate_second(0, first, range(1, 4)))

    def substitute_second(i, following):
        for kk in reversed(range(4)):
            k = at(SLOTS - 1 - i, kk)
            following = val_m[k, :] - ratio_m[k, :] * following
        return following

    bottom = jnp.where(ice[0], lax.fori_loop(0, SLOTS, substitute_second, zero), 0.0)

    product = w2[0:8, :] * bottom
    gradient = -bed[0][0:4, :] * (product[0:4, :] + product[4:8, :])
    grad[...] = gradient
    remote(grad, grad_in, grad_send, grad_recv, (bm, bl))

    lane1 = lax.broadcasted_iota(jnp.int32, (1, 128), 1)
    grad_row = jnp.sum(gradient * gradient, axis=0, keepdims=True)
    fit_row = jnp.sum(0.5 * mismatch[0] * mismatch[0], axis=0, keepdims=True)
    grad_row = grad_row + pltpu.roll(grad_row, 64, 1)
    fit_row = fit_row + pltpu.roll(fit_row, 64, 1)
    row = jnp.where(lane1 < 64, grad_row, fit_row)
    for number, (me, others, peer, row_ref, sum_ref, send_sem, recv_sem) in enumerate(stages):
        row_ref[...] = row
        sum_ref[me] = row
        for i, other in enumerate(others):
            remote(row_ref, sum_ref.at[me], send_sem.at[i], recv_sem.at[me], peer(other))
        if number == 0:
            for l in range(SLOTS):
                remote(
                    w2.at[l * SLAB:l * SLAB + 32], vel_in.at[pl.ds(pl.multiple_of(bl * SLAB, 8), 32)],
                    vel_send.at[l], vel_recv.at[bl], holders[l],
                )
        else:
            for l in range(SLOTS):
                arrived(vel_in.at[l * SLAB:l * SLAB + 32], vel_recv.at[l])
            for c in range(2):
                for kk in range(4):
                    for s in range(4):
                        piece = vel_in[pl.ds(kk * 8 + c * 4 + s, 8, stride=SLAB), :]
                        vout[pl.ds((c * 4 + kk) * 32 + s, 8, stride=4), :] = piece
        for other in reversed(others):
            arrived(sum_ref.at[other], recv_sem.at[other])
        parts = [sum_ref[i] for i in range(32)]
        while len(parts) > 1:
            parts = [parts[i] + parts[i + 1] for i in range(0, len(parts), 2)]
        row = parts[0]

    grad_total = jnp.sum(jnp.where(lane1 < 64, row, 0.0))
    fit_total = jnp.sum(jnp.where(lane1 < 64, 0.0, row))
    misfit_out[...] = jnp.full((1, 128), fit_total, f32) / COLUMNS
    arrived(grad_in, grad_recv)
    scale = jnp.sqrt(jnp.full((4, 128), grad_total, f32) / COLUMNS + 1e-06)
    fric_out[...] = logf[...] - step_size * grad_in[...] / scale

    for copy in sends:
        copy.wait_send()
    bulk += [(w0, halo_send.at[0, i]) for i in range(2)]
    for src, sem in bulk:
        arrived(src, sem)


def hand_over(out, fric, misfit, out_hbm, fric_hbm, misfit_hbm, sem):
    copies = [
        pltpu.make_async_copy(src, dst, sem.at[i])
        for i, (src, dst) in enumerate(((out, out_hbm), (fric, fric_hbm), (misfit, misfit_hbm)))
    ]
    for copy in copies:
        copy.start()
    for copy in copies:
        copy.wait()


def on_device(velocity_init, driving, observed, log_friction, ice_mask):
    vel = velocity_init.reshape(2, 4, 2, 16, 128).transpose(0, 1, 3, 2, 4).reshape(256, 128)

    def tiles(a, lead):
        b = a.reshape(lead, 2, 2, 128).transpose(0, 2, 1, 3)
        return b.reshape(lead * 4, 128)

    full, half, slab = (256, 128), (128, 128), (SLOTS * SLAB, 128)
    vm = lambda shape: pltpu.VMEM(shape, f32)
    dma = pltpu.SemaphoreType.DMA
    scratch = [vm((272, 128)), vm((8, 128)), vm((8, 128)), vm((4, 128)), pltpu.VMEM((4, 128), jnp.int32)]
    scratch += [vm(slab), vm((24, 128)), vm((3, 24, 128))]
    scratch += [vm(slab)] * 8 + [vm(half)] * 4
    scratch += [vm(slab)] * 13 + [vm((GROUPS, 16, 8, 128))]
    scratch += [vm(slab), vm((4, 128)), vm((4, 128))]
    scratch += [vm((1, 128))] * 2 + [vm((32, 1, 128))] * 2
    scratch += [dma((5,)), dma((8,)), dma((8,)), dma((3,)), dma((3,)), dma((3, 2)), dma((3, 2))]
    scratch += [dma((8,)), dma((8,)), dma, dma] + [dma((32,))] * 4 + [pltpu.SemaphoreType.REGULAR((6,))]
    anywhere = pl.BlockSpec(memory_space=pl.ANY)
    out, fric, misfit = pl.pallas_call(
        kernel,
        out_shape=(
            pltpu.VMEM(full, f32),
            pltpu.VMEM((4, 128), f32),
            pltpu.VMEM((1, 128), f32),
        ),
        in_specs=[anywhere] * 5,
        out_specs=(
            pl.BlockSpec(memory_space=pltpu.VMEM),
            pl.BlockSpec(memory_space=pltpu.VMEM),
            pl.BlockSpec(memory_space=pltpu.VMEM),
        ),
        scratch_shapes=scratch,
        compiler_params=pltpu.CompilerParams(collective_id=0, has_side_effects=True),
    )(vel, tiles(driving, 2), tiles(observed, 2), tiles(log_friction, 1), tiles(ice_mask, 1))
    out, fric, misfit = pl.pallas_call(
        hand_over,
        out_shape=(
            jax.ShapeDtypeStruct(full, f32),
            jax.ShapeDtypeStruct((4, 128), f32),
            jax.ShapeDtypeStruct((1, 128), f32),
        ),
        in_specs=[pl.BlockSpec(memory_space=pltpu.VMEM)] * 3,
        out_specs=(anywhere,) * 3,
        scratch_shapes=[dma((3,))],
    )(*(pltpu.with_memory_space_constraint(a, pltpu.VMEM) for a in (out, fric, misfit)))
    velocity = out.reshape(2, 4, 16, 2, 128).transpose(0, 1, 3, 2, 4).reshape(2, 4, 2, 2048)
    fric = fric.reshape(2, 2, 128).transpose(1, 0, 2).reshape(2, 256)
    return velocity, fric, misfit[0, 0]


def solution(mesh):
    in_specs = (
        P(None, "layer", "map", None),
        P(None, "map", "layer"),
        P(None, "map", "layer"),
        P("map", "layer"),
        P("map", "layer"),
    )
    out_specs = (P(None, "layer", "map", None), P("map", "layer"), P())
    return jax.shard_map(on_device, mesh=mesh, in_specs=in_specs, out_specs=out_specs, check_vma=False)
```

```python
import jax
import jax.numpy as jnp
from jax import lax
from jax.experimental import pallas as pl
from jax.experimental.pallas import tpu as pltpu
from jax.sharding import PartitionSpec as P

strain_floor = 0.1
step_size = 0.5
LAYERS = 32
SLOTS = 8
BLOCKS = 128
GROUPS = 4
COLUMNS = 256 * 2048
MESH = pl.DeviceIdType.MESH
f32 = jnp.float32

SLAB = 40


def place(m):
    return lax.div(m, 8), lax.rem(lax.div(m, 2), 4), lax.rem(m, 2)


def device_at(x, y, z, core):
    return ((z * 4 + lax.rem(y, 4)) * 2 + core, x * 2 + lax.div(y, 4))


def owner_of(m, l):
    z, y_lo, core = place(m)
    y = lax.rem(l, 2) * 4 + y_lo
    odd = lax.rem(z, 2)
    return device_at(lax.div(l, 2), lax.rem(odd * (y + 2) + (1 - odd) * (13 - y), 8), z, core)


def block_of(x, y, z, core):
    odd = lax.rem(z, 2)
    return device_at(x, lax.rem(odd * (y + 6) + (1 - odd) * (13 - y), 8), z, core)


def kernel(
    vel_hbm, drv_hbm, obs_hbm, logf_hbm, mask_hbm,
    vout, fric_out, misfit_out,
    vin, drv, obs, logf, mask, stage, small, small_in,
    w0, w1, w2, dn0, up0, dn1, up1, am, adn, aup, alow, ahigh,
    eta_m, eta_r, diag_m, diag_r, rhs_m, rhs_r, ratio_m, ratio_r, val_m, val_r, inv_m, inv_r, rim_x, faces, cross, flip,
    vel_in, grad, grad_in, row1, row2, sum1, sum2,
    load_sem, a2a_send, a2a_recv, small_send, small_recv, halo_send, halo_recv,
    vel_send, vel_recv, grad_send, grad_recv, s1_send, s1_recv, s2_send, s2_recv, token,
):
    loads = [
        pltpu.make_async_copy(src, dst, load_sem.at[i])
        for i, (src, dst) in enumerate(
            ((vel_hbm, vin.at[8:264]), (drv_hbm, drv), (obs_hbm, obs), (logf_hbm, logf), (mask_hbm, mask))
        )
    ]
    for load in loads:
        load.start()

    M = lax.axis_index("map")
    L = lax.axis_index("layer")
    z, y_lo, core = place(M)
    x = lax.div(L, 2)
    y = lax.rem(L, 2) * 4 + y_lo
    bm, bl = block_of(x, y, z, core)
    below = owner_of(lax.rem(bm + BLOCKS - 1, BLOCKS), bl)
    above = owner_of(lax.rem(bm + 1, BLOCKS), bl)
    owners = [owner_of(M, jnp.int32(l)) for l in range(SLOTS)]
    holders = [(bm, jnp.int32(l)) for l in range(SLOTS)]

    def peer_z(j):
        return device_at(x, y, lax.div(j, 2), lax.rem(j, 2))

    def peer_xy(j):
        return device_at(lax.div(j, 8), lax.rem(j, 8), z, core)

    ring_z = sorted(((dz, dc) for dz in range(16) for dc in range(2)), key=lambda d: -min(d[0], 16 - d[0]) - d[1] / 2)[:-1]
    ring_xy = sorted(((dx, dy) for dx in range(4) for dy in range(8)), key=lambda d: -min(d[0], 4 - d[0]) - min(d[1], 8 - d[1]))[:-1]
    zs = [lax.rem(z + dz, 16) for dz in range(16)]
    xs = [lax.rem(x + dx, 4) for dx in range(4)]
    ys = [lax.rem(y + dy, 8) for dy in range(8)]
    stages = (
        (z * 2 + core, [zs[dz] * 2 + (1 - core if dc else core) for dz, dc in ring_z], peer_z, row1, sum1, s1_send, s1_recv),
        (x * 8 + y, [xs[dx] * 8 + ys[dy] for dx, dy in ring_xy], peer_xy, row2, sum2, s2_send, s2_recv),
    )

    def along_z(far):
        return device_at(x, y, lax.rem(far, 16), core)

    partners = owners + holders + [below, above, along_z(z + 1), along_z(z + 15)]
    barrier = pltpu.get_barrier_semaphore()
    for partner in partners:
        pl.semaphore_signal(barrier, inc=1, device_id=partner, device_id_type=MESH)

    for load in loads[1:]:
        load.wait()
    small[0:8, :] = drv[...]
    small[8:16, :] = obs[...]
    small[16:20, :] = jnp.exp(logf[...]) * (mask[...] == 1).astype(f32)
    small[20:24, :] = (mask[...] != 0).astype(f32)
    loads[0].wait()

    lane2 = lax.broadcasted_iota(jnp.int32, (2, 128), 1)
    lane8 = lax.broadcasted_iota(jnp.int32, (8, 128), 1)
    row8 = lax.broadcasted_iota(jnp.int32, (8, 128), 0)
    zero = jnp.zeros((8, 128), f32)

    def turn(v):
        return pltpu.roll(v, 64, 1)

    def pack(right_a, left_a, right_b, left_b):
        low = jnp.where(lane8 < 32, right_a, turn(left_a))
        return jnp.where(lane8 < 64, low, jnp.where(lane8 < 96, turn(right_b), left_b))

    for c in range(2):
        for kk in range(4):
            for s in range(4):
                stage[pl.ds(kk * 8 + c * 4 + s, 8, stride=SLAB), :] = vin[pl.ds(8 + (c * 4 + kk) * 32 + s, 8, stride=4), :]
        for q in range(2):
            for r in range(2):
                sides = []
                for kk in (2 * q, 2 * q + 1):
                    first = 8 + (c * 4 + kk) * 32 + r
                    sides.append(jnp.where(row8 < SLOTS - 1, vin[pl.ds(first + 4, 8, stride=4), :], 0.0))
                    sides.append(jnp.where(row8 > 0, vin[pl.ds(first - 2, 8, stride=4), :], 0.0))
                stage[pl.ds(32 + q * 4 + c * 2 + r, 8, stride=SLAB), :] = pack(*sides)

    pl.semaphore_wait(barrier, len(partners))

    def give_tokens(level):
        for way, far in ((0, z + (1 << level)), (1, z + 16 - (1 << level))):
            pl.semaphore_signal(token.at[level * 2 + way], inc=1, device_id=along_z(far), device_id_type=MESH)

    def take_tokens(level):
        for way in range(2):
            pl.semaphore_wait(token.at[level * 2 + way], 1)

    give_tokens(0)
    sends = []

    def remote(src, dst, send_sem, recv_sem, device):
        copy = pltpu.make_async_remote_copy(
            src_ref=src, dst_ref=dst, send_sem=send_sem, recv_sem=recv_sem, device_id=device, device_id_type=MESH
        )
        copy.start()
        sends.append(copy)

    bulk = []

    def pieces(src, dst, count, index, device):
        size = src.shape[0] // count
        for i in reversed(range(count)):
            rows = pl.ds(i * size, size)
            pltpu.make_async_remote_copy(
                src_ref=src.at[rows], dst_ref=dst.at[rows], send_sem=halo_send.at[index],
                recv_sem=halo_recv.at[index], device_id=device, device_id_type=MESH,
            ).start()
        bulk.append((src, halo_send.at[index]))

    def arrived(ref, sem):
        pltpu.make_async_copy(ref, ref, sem).wait()

    rows = pl.ds(pl.multiple_of(L * SLAB, 8), SLAB)
    def slots_by_x(order):
        return [lax.rem(x + dx, 4) * 2 + half for dx in order for half in range(2)]

    for l in slots_by_x((2, 1, 3, 0)):
        part = pl.ds(pl.multiple_of(l * SLAB, 8), SLAB)
        remote(stage.at[part], w0.at[rows], a2a_send.at[l], a2a_recv.at[L], owner_of(M, l))
    for side in range(3):
        target = owner_of(M, lax.rem(L + SLOTS + 1 - side, SLOTS))
        remote(small, small_in.at[side], small_send.at[side], small_recv.at[side], target)

    take_tokens(0)
    give_tokens(1)
    for l in slots_by_x((0, 1, 3, 2)):
        rows = pl.ds(pl.multiple_of(l * SLAB, 8), SLAB)
        arrived(w0.at[rows], a2a_recv.at[l])
        for i, (device, land) in enumerate(((below, up0), (above, dn0))):
            pltpu.make_async_remote_copy(
                src_ref=w0.at[rows], dst_ref=land.at[rows], send_sem=halo_send.at[0, i],
                recv_sem=halo_recv.at[0, i], device_id=device, device_id_type=MESH,
            ).start()

    take_tokens(1)
    give_tokens(2)
    for side in range(3):
        arrived(small_in.at[side], small_recv.at[side])
    has_left = (bl > 0).astype(f32)
    has_right = (bl < SLOTS - 1).astype(f32)
    has_below = (bm > 0).astype(f32)
    has_above = (bm < BLOCKS - 1).astype(f32)

    def double(rows):
        return jnp.concatenate([rows, rows], 0)

    def rim_rows(start, comps):
        parts = []
        for c in range(comps):
            at = start + 4 * c
            parts.append(jnp.where(lane2 < 64, small_in[2, at:at + 2, :] * has_right, small_in[0, at + 2:at + 4, :] * has_left))
        if comps == 1:
            parts = parts * 2
        return double(jnp.concatenate(parts, 0))

    drive = (small_in[1, 0:8, :], rim_rows(0, 2))
    seen = (small_in[1, 8:16, :], rim_rows(8, 2))
    bed = (double(small_in[1, 16:20, :]), rim_rows(16, 1))
    ice = (double(small_in[1, 20:24, :]) > 0.5, rim_rows(20, 1) > 0.5)

    def ahead(tiles):
        turned = [pltpu.roll(t, 127, 1) for t in tiles]
        return [jnp.where(lane8 == 127, turned[(i + 1) % 3], turned[i]) for i in range(3)]

    def behind(tiles):
        turned = [pltpu.roll(t, 1, 1) for t in tiles]
        return [jnp.where(lane8 == 0, turned[(i + 2) % 3], turned[i]) for i in range(3)]

    def load_tiles(slab, c, r, kk, packed):
        tiles = [slab[pl.ds(kk * 8 + c * 4 + t * 2 + r, 8, stride=SLAB), :] for t in range(2)]
        return tiles + [packed[kk % 2]]

    def unpack(slab, c, r, q):
        v = slab[pl.ds(32 + q * 4 + c * 2 + r, 8, stride=SLAB), :]
        turned = turn(v)
        return jnp.where(lane8 < 64, v, turned), jnp.where(lane8 < 64, turned, v)

    def store_tile(main, rim, kk, c, t, r, value):
        if t < 2:
            main[pl.ds(kk * 8 + c * 4 + t * 2 + r, 8, stride=SLAB), :] = value
        else:
            rim[pl.ds(kk * 8 + c * 2 + r, 8, stride=SLAB), :] = value

    def scaled(tiles, factor):
        return [t * factor for t in tiles]

    def forward_terms(own, low, high):
        for q in range(2):
            rims = [[unpack(slab, c, r, q) for slab in (low, own, high) for r in range(2)] for c in range(2)]
            for kk in (2 * q, 2 * q + 1):
                group(own, low, high, kk, rims)

    def group(own, low, high, kk, rims):
        w = []
        for c in range(2):
            rows = [scaled(load_tiles(low, c, r, kk, rims[c][r]), has_below) for r in range(2)]
            rows += [load_tiles(own, c, r, kk, rims[c][2 + r]) for r in range(2)]
            rows += [scaled(load_tiles(high, c, r, kk, rims[c][4 + r]), has_above) for r in range(2)]
            w.append(rows)
        right = [[ahead(w[c][r]) for r in range(1, 5)] for c in range(2)]
        left = [[behind(w[c][r]) for r in range(1, 5)] for c in range(2)]
        eta = []
        for r in range(4):
            tiles = []
            for t in range(3):
                u_x = (w[0][r + 2][t] - w[0][r][t]) * 0.5
                v_x = (w[1][r + 2][t] - w[1][r][t]) * 0.5
                u_y = (right[0][r][t] - left[0][r][t]) * 0.5
                v_y = (right[1][r][t] - left[1][r][t]) * 0.5
                shear = u_y + v_x
                rate = u_x * u_x + v_y * v_y + u_x * v_y + 0.25 * shear * shear
                tiles.append(jnp.exp(jnp.log(strain_floor + rate) * (-1.0 / 3.0)))
            eta.append(tiles)
        for r in range(2):
            eta_right, eta_left = ahead(eta[r + 1]), behind(eta[r + 1])
            for t in range(3):
                centre = eta[r + 1][t]
                east = 0.5 * (centre + eta[r + 2][t])
                west = 0.5 * (centre + eta[r][t])
                north = 0.5 * (centre + eta_right[t])
                south = 0.5 * (centre + eta_left[t])
                along, across = east + west, north + south
                if t < 2:
                    for i, face in enumerate((east, west, north, south)):
                        faces[kk, (r * 2 + t) * 4 + i] = face
                u, v = w
                sum_u = (
                    4.0 * (east * u[r + 3][t] + west * u[r + 1][t])
                    + north * right[0][r + 1][t] + south * left[0][r + 1][t]
                )
                sum_v = (
                    east * v[r + 3][t] + west * v[r + 1][t]
                    + 4.0 * (north * right[1][r + 1][t] + south * left[1][r + 1][t])
                )
                store_tile(eta_m, eta_r, kk, 0, t, r, centre)
                store_tile(eta_m, eta_r, kk, 1, t, r, centre)
                store_tile(diag_m, diag_r, kk, 0, t, r, 4.0 * along + across)
                store_tile(diag_m, diag_r, kk, 1, t, r, along + 4.0 * across)
                store_tile(rhs_m, rhs_r, kk, 0, t, r, sum_u)
                store_tile(rhs_m, rhs_r, kk, 1, t, r, sum_v)

    pairs = (
        (eta_m, diag_m, rhs_m, ratio_m, val_m, inv_m),
        (eta_r, diag_r, rhs_r, ratio_r, val_r, inv_r),
    )

    def at(slot, kk):
        return pl.ds(pl.multiple_of(slot * SLAB + kk * 8, 8), 8)

    def solve(out):
        def eliminate(slot, carry, last=False):
            for kk in range(4):
                new = []
                for part in range(2):
                    eta, diag, rhs, ratio, val, inv = pairs[part]
                    lower, ratio_prev, val_prev, pad = carry[part]
                    k = at(slot, kk)
                    if last and kk == 3:
                        upper = zero
                    else:
                        upper = 1024.0 * (eta[k, :] + eta[at(slot, kk + 1) if kk < 3 else at(slot + 1, 0), :])
                    inverse = 1.0 / (((lower + upper + pad) + diag[k, :]) + lower * ratio_prev)
                    ratio_now = -upper * inverse
                    val_now = (drive[part] + rhs[k, :] + lower * val_prev) * inverse
                    ratio[k, :] = ratio_now
                    val[k, :] = val_now
                    inv[k, :] = inverse
                    new.append((upper, ratio_now, val_now, zero))
                carry = tuple(new)
            return carry

        carry = tuple((zero, zero, zero, bed[part]) for part in range(2))
        carry = lax.fori_loop(0, SLOTS - 1, eliminate, carry)
        eliminate(SLOTS - 1, carry, last=True)

        def substitute(i, following):
            slot = SLOTS - 1 - i
            for kk in reversed(range(4)):
                k = at(slot, kk)
                new = []
                for part, to in enumerate((out, rim_x)):
                    ratio, val = pairs[part][3], pairs[part][4]
                    now = val[k, :] - ratio[k, :] * following[part]
                    to[k, :] = jnp.where(ice[part], now, 0.0)
                    new.append(now)
                following = tuple(new)
            return following

        lax.fori_loop(0, SLOTS, substitute, (zero, zero))

    def pack_rims(out):
        for q in range(2):
            for s in range(4):
                a = rim_x[pl.ds(2 * q * 8 + s, 8, stride=SLAB), :]
                b = rim_x[pl.ds((2 * q + 1) * 8 + s, 8, stride=SLAB), :]
                out[pl.ds(32 + q * 4 + s, 8, stride=SLAB), :] = pack(a, a, b, b)

    for i, land in enumerate((up0, dn0)):
        arrived(land, halo_recv.at[0, i])
    forward_terms(w0, dn0, up0)
    solve(w1)
    pack_rims(w1)
    for i, (device, land) in enumerate(((below, up1), (above, dn1))):
        pieces(w1, land, SLOTS, (1, i), device)

    for i, land in enumerate((up1, dn1)):
        arrived(land, halo_recv.at[1, i])
    forward_terms(w1, dn1, up1)
    solve(w2)
    take_tokens(2)

    top = pl.ds((SLOTS - 1) * SLAB + 24, 8)
    tops = (w2[top, :], rim_x[top, :])
    mismatch = [jnp.where(ice[part], tops[part] - seen[part], 0.0) for part in range(2)]
    source = [float(LAYERS) * mismatch[part] for part in range(2)]
    starts = tuple(source[part] * pairs[part][5][top, :] for part in range(2))
    adjoints = (am, rim_x)
    for part in range(2):
        adjoints[part][top, :] = jnp.where(ice[part], starts[part], 0.0)

    def substitute_first(slot, following, steps=range(4)):
        for kk in reversed(steps):
            k = at(slot, kk)
            new = []
            for part in range(2):
                now = -pairs[part][3][k, :] * following[part]
                adjoints[part][k, :] = jnp.where(ice[part], now, 0.0)
                new.append(now)
            following = tuple(new)
        return following

    following = substitute_first(SLOTS - 1, starts, range(3))
    lax.fori_loop(1, SLOTS, lambda i, carry: substitute_first(SLOTS - 1 - i, carry), following)
    for r, (edge, land, device) in enumerate(((alow, aup, below), (ahigh, adn, above))):
        for s in range(4):
            for j in range(GROUPS):
                edge[pl.ds(j * 32 + s, 8, stride=4), :] = am[pl.ds(j * 8 + s * 2 + r, 8, stride=SLAB), :]
        pieces(edge, land, 4, (2, r), device)

    def eliminate_unit(slot, prev, steps=range(4)):
        for kk in steps:
            k, under = at(slot, kk), at(slot, kk - 1) if kk > 0 else at(slot - 1, 3)
            prev = (1024.0 * (eta_m[under, :] + eta_m[k, :]) * inv_m[k, :]) * prev
            val_m[k, :] = prev
        return prev

    first = inv_m[0:8, :]
    val_m[0:8, :] = first
    lax.fori_loop(1, SLOTS, eliminate_unit, eliminate_unit(0, first, range(1, 4)))

    def substitute_unit(i, following):
        for kk in reversed(range(4)):
            k = at(SLOTS - 1 - i, kk)
            following = val_m[k, :] - ratio_m[k, :] * following
            val_m[k, :] = following
        return following

    lax.fori_loop(0, SLOTS, substitute_unit, zero)
    total = [zero] * 8
    for kk in range(4):
        for c in range(2):
            rows = [[am[pl.ds(kk * 8 + c * 4 + t * 2 + r, 8, stride=SLAB), :] for t in range(2)] for r in range(2)]
            for r in range(2):
                rows[r].append(rim_x[pl.ds(kk * 8 + c * 2 + r, 8, stride=SLAB), :])
            for r in range(2):
                right, left = ahead(rows[r]), behind(rows[r])
                for t in range(2):
                    s = c * 4 + t * 2 + r
                    weight = val_m[pl.ds(kk * 8 + s, 8, stride=SLAB), :]
                    east, west, north, south = [faces[kk, (r * 2 + t) * 4 + i] for i in range(4)]
                    if r == 0:
                        along, outer = east * rows[1][t], west * has_below
                    else:
                        along, outer = west * rows[0][t], east * has_above
                    across = north * right[t] + south * left[t]
                    value = 4.0 * along + across if c == 0 else along + 4.0 * across
                    total[s] = total[s] + weight * value
                    cross[kk, s] = weight * (4.0 * outer if c == 0 else outer)
    ahead_part = val_m[top, :] * source[0]

    arrived(aup, halo_recv.at[2, 0])
    arrived(adn, halo_recv.at[2, 1])
    for s in range(8):
        edge = adn if s % 2 == 0 else aup
        for kk in range(4):
            total[s] = total[s] + cross[kk, s] * edge[pl.ds(kk * 32 + s // 2, 8, stride=4), :]
        flip[s * 8:s * 8 + 8, :] = total[s]
    bottom = ahead_part
    for i in range(8):
        bottom = bottom + flip[pl.ds(i, 8, stride=8), :]
    bottom = jnp.where(ice[0], bottom, 0.0)

    product = w2[0:8, :] * bottom
    gradient = -bed[0][0:4, :] * (product[0:4, :] + product[4:8, :])
    grad[...] = gradient
    remote(grad, grad_in, grad_send, grad_recv, (bm, bl))

    lane1 = lax.broadcasted_iota(jnp.int32, (1, 128), 1)
    grad_row = jnp.sum(gradient * gradient, axis=0, keepdims=True)
    fit_row = jnp.sum(0.5 * mismatch[0] * mismatch[0], axis=0, keepdims=True)
    grad_row = grad_row + pltpu.roll(grad_row, 64, 1)
    fit_row = fit_row + pltpu.roll(fit_row, 64, 1)
    row = jnp.where(lane1 < 64, grad_row, fit_row)
    for number, (me, others, peer, row_ref, sum_ref, send_sem, recv_sem) in enumerate(stages):
        row_ref[...] = row
        sum_ref[me] = row
        for i, other in enumerate(others):
            remote(row_ref, sum_ref.at[me], send_sem.at[i], recv_sem.at[me], peer(other))
        if number == 0:
            for l in range(SLOTS):
                remote(
                    w2.at[l * SLAB:l * SLAB + 32], vel_in.at[pl.ds(pl.multiple_of(bl * SLAB, 8), 32)],
                    vel_send.at[l], vel_recv.at[bl], holders[l],
                )
        else:
            for l in range(SLOTS):
                arrived(vel_in.at[l * SLAB:l * SLAB + 32], vel_recv.at[l])
            for c in range(2):
                for kk in range(4):
                    for s in range(4):
                        piece = vel_in[pl.ds(kk * 8 + c * 4 + s, 8, stride=SLAB), :]
                        vout[pl.ds((c * 4 + kk) * 32 + s, 8, stride=4), :] = piece
        if number == 1:
            for copy in sends:
                copy.wait_send()
            bulk += [(w0, halo_send.at[0, i]) for i in range(2)]
            for src, sem in bulk:
                arrived(src, sem)
        for other in reversed(others):
            arrived(sum_ref.at[other], recv_sem.at[other])
        parts = [sum_ref[i] for i in range(32)]
        while len(parts) > 1:
            parts = [parts[i] + parts[i + 1] for i in range(0, len(parts), 2)]
        row = parts[0]

    grad_total = jnp.sum(jnp.where(lane1 < 64, row, 0.0))
    fit_total = jnp.sum(jnp.where(lane1 < 64, 0.0, row))
    misfit_out[...] = jnp.full((1, 128), fit_total, f32) / COLUMNS
    arrived(grad_in, grad_recv)
    scale = jnp.sqrt(jnp.full((4, 128), grad_total, f32) / COLUMNS + 1e-06)
    fric_out[...] = logf[...] - step_size * grad_in[...] / scale


def hand_over(out, fric, misfit, out_hbm, fric_hbm, misfit_hbm, sem):
    copies = [
        pltpu.make_async_copy(src, dst, sem.at[i])
        for i, (src, dst) in enumerate(((out, out_hbm), (fric, fric_hbm), (misfit, misfit_hbm)))
    ]
    for copy in copies:
        copy.start()
    for copy in copies:
        copy.wait()


def on_device(velocity_init, driving, observed, log_friction, ice_mask):
    vel = velocity_init.reshape(2, 4, 2, 16, 128).transpose(0, 1, 3, 2, 4).reshape(256, 128)

    def tiles(a, lead):
        b = a.reshape(lead, 2, 2, 128).transpose(0, 2, 1, 3)
        return b.reshape(lead * 4, 128)

    full, half, slab = (256, 128), (128, 128), (SLOTS * SLAB, 128)
    vm = lambda shape: pltpu.VMEM(shape, f32)
    dma = pltpu.SemaphoreType.DMA
    scratch = [vm((272, 128)), vm((8, 128)), vm((8, 128)), vm((4, 128)), pltpu.VMEM((4, 128), jnp.int32)]
    scratch += [vm(slab), vm((24, 128)), vm((3, 24, 128))]
    scratch += [vm(slab)] * 8 + [vm(half)] * 4
    scratch += [vm(slab)] * 13 + [vm((GROUPS, 16, 8, 128)), vm((GROUPS, 8, 8, 128)), vm((64, 128))]
    scratch += [vm(slab), vm((4, 128)), vm((4, 128))]
    scratch += [vm((1, 128))] * 2 + [vm((32, 1, 128))] * 2
    scratch += [dma((5,)), dma((8,)), dma((8,)), dma((3,)), dma((3,)), dma((3, 2)), dma((3, 2))]
    scratch += [dma((8,)), dma((8,)), dma, dma] + [dma((32,))] * 4 + [pltpu.SemaphoreType.REGULAR((6,))]
    anywhere = pl.BlockSpec(memory_space=pl.ANY)
    out, fric, misfit = pl.pallas_call(
        kernel,
        out_shape=(
            pltpu.VMEM(full, f32),
            pltpu.VMEM((4, 128), f32),
            pltpu.VMEM((1, 128), f32),
        ),
        in_specs=[anywhere] * 5,
        out_specs=(
            pl.BlockSpec(memory_space=pltpu.VMEM),
            pl.BlockSpec(memory_space=pltpu.VMEM),
            pl.BlockSpec(memory_space=pltpu.VMEM),
        ),
        scratch_shapes=scratch,
        compiler_params=pltpu.CompilerParams(collective_id=0, has_side_effects=True),
    )(vel, tiles(driving, 2), tiles(observed, 2), tiles(log_friction, 1), tiles(ice_mask, 1))
    out, fric, misfit = pl.pallas_call(
        hand_over,
        out_shape=(
            jax.ShapeDtypeStruct(full, f32),
            jax.ShapeDtypeStruct((4, 128), f32),
            jax.ShapeDtypeStruct((1, 128), f32),
        ),
        in_specs=[pl.BlockSpec(memory_space=pltpu.VMEM)] * 3,
        out_specs=(anywhere,) * 3,
        scratch_shapes=[dma((3,))],
    )(*(pltpu.with_memory_space_constraint(a, pltpu.VMEM) for a in (out, fric, misfit)))
    velocity = out.reshape(2, 4, 16, 2, 128).transpose(0, 1, 3, 2, 4).reshape(2, 4, 2, 2048)
    fric = fric.reshape(2, 2, 128).transpose(1, 0, 2).reshape(2, 256)
    return velocity, fric, misfit[0, 0]


def solution(mesh):
    in_specs = (
        P(None, "layer", "map", None),
        P(None, "map", "layer"),
        P(None, "map", "layer"),
        P("map", "layer"),
        P("map", "layer"),
    )
    out_specs = (P(None, "layer", "map", None), P("map", "layer"), P())
    return jax.shard_map(on_device, mesh=mesh, in_specs=in_specs, out_specs=out_specs, check_vma=False)
```

```python
import jax
import jax.numpy as jnp
from jax import lax
from jax.experimental import pallas as pl
from jax.experimental.pallas import tpu as pltpu
from jax.sharding import PartitionSpec as P

strain_floor = 0.1
step_size = 0.5
LAYERS = 32
SLOTS = 8
BLOCKS = 128
GROUPS = 4
COLUMNS = 256 * 2048
MESH = pl.DeviceIdType.MESH
f32 = jnp.float32

SLAB = 40


def place(m):
    return lax.div(m, 8), lax.rem(lax.div(m, 2), 4), lax.rem(m, 2)


def device_at(x, y, z, core):
    return ((z * 4 + lax.rem(y, 4)) * 2 + core, x * 2 + lax.div(y, 4))


def owner_of(m, l):
    z, y_lo, core = place(m)
    y = lax.rem(l, 2) * 4 + y_lo
    odd = lax.rem(z, 2)
    return device_at(lax.div(l, 2), lax.rem((1 - odd) * (y + 2) + odd * (13 - y), 8), z, core)


def block_of(x, y, z, core):
    odd = lax.rem(z, 2)
    return device_at(x, lax.rem((1 - odd) * (y + 6) + odd * (13 - y), 8), z, core)


def kernel(
    vel_hbm, drv_hbm, obs_hbm, logf_hbm, mask_hbm,
    vout, fric_out, misfit_out,
    vin, drv, obs, logf, mask, stage, small, small_in,
    w0, w1, w2, dn0, up0, dn1, up1, am, adn, aup, alow, ahigh,
    eta_m, eta_r, diag_m, diag_r, rhs_m, rhs_r, ratio_m, ratio_r, val_m, val_r, inv_m, inv_r, rim_x, faces, cross, flip,
    vel_in, grad, grad_in, row1, row2, sum1, sum2,
    load_sem, a2a_send, a2a_recv, small_send, small_recv, halo_send, halo_recv,
    vel_send, vel_recv, grad_send, grad_recv, s1_send, s1_recv, s2_send, s2_recv, token,
):
    loads = [
        pltpu.make_async_copy(src, dst, load_sem.at[i])
        for i, (src, dst) in enumerate(
            ((vel_hbm, vin.at[8:264]), (drv_hbm, drv), (obs_hbm, obs), (logf_hbm, logf), (mask_hbm, mask))
        )
    ]
    for load in loads:
        load.start()

    M = lax.axis_index("map")
    L = lax.axis_index("layer")
    z, y_lo, core = place(M)
    x = lax.div(L, 2)
    y = lax.rem(L, 2) * 4 + y_lo
    bm, bl = block_of(x, y, z, core)
    below = owner_of(lax.rem(bm + BLOCKS - 1, BLOCKS), bl)
    above = owner_of(lax.rem(bm + 1, BLOCKS), bl)
    own_map, own_half = owner_of(M, jnp.int32(0))
    flip_half = 1 - 2 * own_half

    def owner_in_row(column, half):
        return own_map, column * 2 + own_half + half * flip_half

    owners = [owner_in_row(jnp.int32(column), half) for column in range(4) for half in range(2)]
    holders = [(bm, jnp.int32(l)) for l in range(SLOTS)]

    def peer_z(j):
        return device_at(x, y, lax.div(j, 2), lax.rem(j, 2))

    def peer_xy(j):
        return device_at(lax.div(j, 8), lax.rem(j, 8), z, core)

    ring_z = sorted(((dz, dc) for dz in range(16) for dc in range(2)), key=lambda d: -min(d[0], 16 - d[0]) - d[1] / 2)[:-1]
    ring_xy = sorted(((dx, dy) for dx in range(4) for dy in range(8)), key=lambda d: -min(d[0], 4 - d[0]) - min(d[1], 8 - d[1]))[:-1]
    zs = [lax.rem(z + dz, 16) for dz in range(16)]
    xs = [lax.rem(x + dx, 4) for dx in range(4)]
    ys = [lax.rem(y + dy, 8) for dy in range(8)]
    stages = (
        (z * 2 + core, [zs[dz] * 2 + (1 - core if dc else core) for dz, dc in ring_z], peer_z, row1, sum1, s1_send, s1_recv),
        (x * 8 + y, [xs[dx] * 8 + ys[dy] for dx, dy in ring_xy], peer_xy, row2, sum2, s2_send, s2_recv),
    )

    def along_z(far):
        return device_at(x, y, lax.rem(far, 16), core)

    partners = owners + holders + [below, above, along_z(z + 1), along_z(z + 15)]
    barrier = pltpu.get_barrier_semaphore()
    for partner in partners:
        pl.semaphore_signal(barrier, inc=1, device_id=partner, device_id_type=MESH)

    for load in loads[1:]:
        load.wait()
    small[0:8, :] = drv[...]
    small[8:16, :] = obs[...]
    small[16:20, :] = jnp.exp(logf[...]) * (mask[...] == 1).astype(f32)
    small[20:24, :] = (mask[...] != 0).astype(f32)
    loads[0].wait()

    lane2 = lax.broadcasted_iota(jnp.int32, (2, 128), 1)
    lane8 = lax.broadcasted_iota(jnp.int32, (8, 128), 1)
    row8 = lax.broadcasted_iota(jnp.int32, (8, 128), 0)
    zero = jnp.zeros((8, 128), f32)

    def turn(v):
        return pltpu.roll(v, 64, 1)

    def pack(right_a, left_a, right_b, left_b):
        low = jnp.where(lane8 < 32, right_a, turn(left_a))
        return jnp.where(lane8 < 64, low, jnp.where(lane8 < 96, turn(right_b), left_b))

    for c in range(2):
        for kk in range(4):
            for s in range(4):
                stage[pl.ds(kk * 8 + c * 4 + s, 8, stride=SLAB), :] = vin[pl.ds(8 + (c * 4 + kk) * 32 + s, 8, stride=4), :]
        for q in range(2):
            for r in range(2):
                sides = []
                for kk in (2 * q, 2 * q + 1):
                    first = 8 + (c * 4 + kk) * 32 + r
                    sides.append(jnp.where(row8 < SLOTS - 1, vin[pl.ds(first + 4, 8, stride=4), :], 0.0))
                    sides.append(jnp.where(row8 > 0, vin[pl.ds(first - 2, 8, stride=4), :], 0.0))
                stage[pl.ds(32 + q * 4 + c * 2 + r, 8, stride=SLAB), :] = pack(*sides)

    pl.semaphore_wait(barrier, len(partners))

    def give_tokens(level):
        for way, far in ((0, z + (1 << level)), (1, z + 16 - (1 << level))):
            pl.semaphore_signal(token.at[level * 2 + way], inc=1, device_id=along_z(far), device_id_type=MESH)

    def take_tokens(level):
        for way in range(2):
            pl.semaphore_wait(token.at[level * 2 + way], 1)

    give_tokens(0)
    sends = []

    def remote(src, dst, send_sem, recv_sem, device):
        copy = pltpu.make_async_remote_copy(
            src_ref=src, dst_ref=dst, send_sem=send_sem, recv_sem=recv_sem, device_id=device, device_id_type=MESH
        )
        copy.start()
        sends.append(copy)

    bulk = []

    def pieces(src, dst, count, index, device, first, length):
        size = src.shape[0] // count
        for i in reversed(range(count)):
            rows = pl.ds(i * size + first, length)
            pltpu.make_async_remote_copy(
                src_ref=src.at[rows], dst_ref=dst.at[rows], send_sem=halo_send.at[index],
                recv_sem=halo_recv.at[index], device_id=device, device_id_type=MESH,
            ).start()

    def arrived(ref, sem):
        pltpu.make_async_copy(ref, ref, sem).wait()

    rows = pl.ds(pl.multiple_of(L * SLAB, 8), SLAB)
    def slots_by_x(order):
        return [lax.rem(x + dx, 4) * 2 + half for dx in order for half in range(2)]

    for dx in (2, 1, 3, 0):
        column = lax.rem(x + dx, 4)
        for half in range(2):
            l = column * 2 + half
            part = pl.ds(pl.multiple_of(l * SLAB, 8), SLAB)
            remote(stage.at[part], w0.at[rows], a2a_send.at[l], a2a_recv.at[L], owner_in_row(column, half))
    for side in range(3):
        target = owner_of(M, lax.rem(L + SLOTS + 1 - side, SLOTS))
        remote(small, small_in.at[side], small_send.at[side], small_recv.at[side], target)

    take_tokens(0)
    give_tokens(1)
    for l in slots_by_x((0, 1, 3, 2)):
        rows = pl.ds(pl.multiple_of(l * SLAB, 8), SLAB)
        arrived(w0.at[rows], a2a_recv.at[l])
        for i, (device, land) in enumerate(((below, up0), (above, dn0))):
            pltpu.make_async_remote_copy(
                src_ref=w0.at[rows], dst_ref=land.at[rows], send_sem=halo_send.at[0, i],
                recv_sem=halo_recv.at[0, i], device_id=device, device_id_type=MESH,
            ).start()

    take_tokens(1)
    give_tokens(2)
    for side in range(3):
        arrived(small_in.at[side], small_recv.at[side])
    has_left = (bl > 0).astype(f32)
    has_right = (bl < SLOTS - 1).astype(f32)
    has_below = (bm > 0).astype(f32)
    has_above = (bm < BLOCKS - 1).astype(f32)

    def double(rows):
        return jnp.concatenate([rows, rows], 0)

    def rim_rows(start, comps):
        parts = []
        for c in range(comps):
            at = start + 4 * c
            parts.append(jnp.where(lane2 < 64, small_in[2, at:at + 2, :] * has_right, small_in[0, at + 2:at + 4, :] * has_left))
        if comps == 1:
            parts = parts * 2
        return double(jnp.concatenate(parts, 0))

    drive = (small_in[1, 0:8, :], rim_rows(0, 2))
    seen = (small_in[1, 8:16, :], rim_rows(8, 2))
    bed = (double(small_in[1, 16:20, :]), rim_rows(16, 1))
    ice = (double(small_in[1, 20:24, :]) > 0.5, rim_rows(20, 1) > 0.5)

    def ahead(tiles):
        turned = [pltpu.roll(t, 127, 1) for t in tiles]
        return [jnp.where(lane8 == 127, turned[(i + 1) % 3], turned[i]) for i in range(3)]

    def behind(tiles):
        turned = [pltpu.roll(t, 1, 1) for t in tiles]
        return [jnp.where(lane8 == 0, turned[(i + 2) % 3], turned[i]) for i in range(3)]

    def load_tiles(slab, c, r, kk, packed):
        tiles = [slab[pl.ds(kk * 8 + c * 4 + t * 2 + r, 8, stride=SLAB), :] for t in range(2)]
        return tiles + [packed[kk % 2]]

    def unpack(slab, c, r, q):
        v = slab[pl.ds(32 + q * 4 + c * 2 + r, 8, stride=SLAB), :]
        turned = turn(v)
        return jnp.where(lane8 < 64, v, turned), jnp.where(lane8 < 64, turned, v)

    def store_tile(main, rim, kk, c, t, r, value):
        if t < 2:
            main[pl.ds(kk * 8 + c * 4 + t * 2 + r, 8, stride=SLAB), :] = value
        else:
            rim[pl.ds(kk * 8 + c * 2 + r, 8, stride=SLAB), :] = value

    def scaled(tiles, factor):
        return [t * factor for t in tiles]

    def forward_terms(own, low, high):
        for q in range(2):
            rims = [[unpack(slab, c, r, q) for slab in (low, own, high) for r in range(2)] for c in range(2)]
            for kk in (2 * q, 2 * q + 1):
                group(own, low, high, kk, rims)

    def group(own, low, high, kk, rims):
        w = []
        for c in range(2):
            rows = [scaled(load_tiles(low, c, r, kk, rims[c][r]), has_below) for r in range(2)]
            rows += [load_tiles(own, c, r, kk, rims[c][2 + r]) for r in range(2)]
            rows += [scaled(load_tiles(high, c, r, kk, rims[c][4 + r]), has_above) for r in range(2)]
            w.append(rows)
        right = [[ahead(w[c][r]) for r in range(1, 5)] for c in range(2)]
        left = [[behind(w[c][r]) for r in range(1, 5)] for c in range(2)]
        eta = []
        for r in range(4):
            tiles = []
            for t in range(3):
                u_x = (w[0][r + 2][t] - w[0][r][t]) * 0.5
                v_x = (w[1][r + 2][t] - w[1][r][t]) * 0.5
                u_y = (right[0][r][t] - left[0][r][t]) * 0.5
                v_y = (right[1][r][t] - left[1][r][t]) * 0.5
                shear = u_y + v_x
                rate = u_x * u_x + v_y * v_y + u_x * v_y + 0.25 * shear * shear
                tiles.append(jnp.exp(jnp.log(strain_floor + rate) * (-1.0 / 3.0)))
            eta.append(tiles)
        for r in range(2):
            eta_right, eta_left = ahead(eta[r + 1]), behind(eta[r + 1])
            for t in range(3):
                centre = eta[r + 1][t]
                east = 0.5 * (centre + eta[r + 2][t])
                west = 0.5 * (centre + eta[r][t])
                north = 0.5 * (centre + eta_right[t])
                south = 0.5 * (centre + eta_left[t])
                along, across = east + west, north + south
                if t < 2:
                    for i, face in enumerate((east, west, north, south)):
                        faces[kk, (r * 2 + t) * 4 + i] = face
                u, v = w
                sum_u = (
                    4.0 * (east * u[r + 3][t] + west * u[r + 1][t])
                    + north * right[0][r + 1][t] + south * left[0][r + 1][t]
                )
                sum_v = (
                    east * v[r + 3][t] + west * v[r + 1][t]
                    + 4.0 * (north * right[1][r + 1][t] + south * left[1][r + 1][t])
                )
                store_tile(eta_m, eta_r, kk, 0, t, r, centre)
                store_tile(eta_m, eta_r, kk, 1, t, r, centre)
                store_tile(diag_m, diag_r, kk, 0, t, r, 4.0 * along + across)
                store_tile(diag_m, diag_r, kk, 1, t, r, along + 4.0 * across)
                store_tile(rhs_m, rhs_r, kk, 0, t, r, sum_u)
                store_tile(rhs_m, rhs_r, kk, 1, t, r, sum_v)

    pairs = (
        (eta_m, diag_m, rhs_m, ratio_m, val_m, inv_m),
        (eta_r, diag_r, rhs_r, ratio_r, val_r, inv_r),
    )

    def at(slot, kk):
        return pl.ds(pl.multiple_of(slot * SLAB + kk * 8, 8), 8)

    def solve(out):
        def eliminate(slot, carry, last=False):
            for kk in range(4):
                new = []
                for part in range(2):
                    eta, diag, rhs, ratio, val, inv = pairs[part]
                    lower, ratio_prev, val_prev, pad = carry[part]
                    k = at(slot, kk)
                    if last and kk == 3:
                        upper = zero
                    else:
                        upper = 1024.0 * (eta[k, :] + eta[at(slot, kk + 1) if kk < 3 else at(slot + 1, 0), :])
                    inverse = 1.0 / (((lower + upper + pad) + diag[k, :]) + lower * ratio_prev)
                    ratio_now = -upper * inverse
                    val_now = (drive[part] + rhs[k, :] + lower * val_prev) * inverse
                    ratio[k, :] = ratio_now
                    val[k, :] = val_now
                    inv[k, :] = inverse
                    new.append((upper, ratio_now, val_now, zero))
                carry = tuple(new)
            return carry

        carry = tuple((zero, zero, zero, bed[part]) for part in range(2))
        carry = lax.fori_loop(0, SLOTS - 1, eliminate, carry)
        eliminate(SLOTS - 1, carry, last=True)

        def substitute(i, following):
            slot = SLOTS - 1 - i
            for kk in reversed(range(4)):
                k = at(slot, kk)
                new = []
                for part, to in enumerate((out, rim_x)):
                    ratio, val = pairs[part][3], pairs[part][4]
                    now = val[k, :] - ratio[k, :] * following[part]
                    to[k, :] = jnp.where(ice[part], now, 0.0)
                    new.append(now)
                following = tuple(new)
            return following

        lax.fori_loop(0, SLOTS, substitute, (zero, zero))

    def pack_rims(out):
        for q in range(2):
            for s in range(4):
                a = rim_x[pl.ds(2 * q * 8 + s, 8, stride=SLAB), :]
                b = rim_x[pl.ds((2 * q + 1) * 8 + s, 8, stride=SLAB), :]
                out[pl.ds(32 + q * 4 + s, 8, stride=SLAB), :] = pack(a, a, b, b)

    for i, land in enumerate((up0, dn0)):
        arrived(land, halo_recv.at[0, i])
    forward_terms(w0, dn0, up0)
    solve(w1)
    for i, (device, land) in enumerate(((below, up1), (above, dn1))):
        pieces(w1, land, SLOTS, (1, i), device, 0, 32)
        bulk.append((w1, halo_send.at[1, i]))
    pack_rims(w1)
    for i, (device, land) in enumerate(((below, up1), (above, dn1))):
        pieces(w1, land, SLOTS, (1, i), device, 32, 8)

    for i, land in enumerate((up1, dn1)):
        arrived(land, halo_recv.at[1, i])
    forward_terms(w1, dn1, up1)
    solve(w2)
    take_tokens(2)

    top = pl.ds((SLOTS - 1) * SLAB + 24, 8)
    tops = (w2[top, :], rim_x[top, :])
    mismatch = [jnp.where(ice[part], tops[part] - seen[part], 0.0) for part in range(2)]
    source = [float(LAYERS) * mismatch[part] for part in range(2)]
    starts = tuple(source[part] * pairs[part][5][top, :] for part in range(2))
    adjoints = (am, rim_x)
    for part in range(2):
        adjoints[part][top, :] = jnp.where(ice[part], starts[part], 0.0)

    def substitute_first(slot, following, steps=range(4)):
        for kk in reversed(steps):
            k = at(slot, kk)
            new = []
            for part in range(2):
                now = -pairs[part][3][k, :] * following[part]
                adjoints[part][k, :] = jnp.where(ice[part], now, 0.0)
                new.append(now)
            following = tuple(new)
        return following

    following = substitute_first(SLOTS - 1, starts, range(3))
    lax.fori_loop(1, SLOTS, lambda i, carry: substitute_first(SLOTS - 1 - i, carry), following)
    for r, (edge, land, device) in enumerate(((alow, aup, below), (ahigh, adn, above))):
        for s in range(4):
            for j in range(GROUPS):
                edge[pl.ds(j * 32 + s, 8, stride=4), :] = am[pl.ds(j * 8 + s * 2 + r, 8, stride=SLAB), :]
        pieces(edge, land, 4, (2, r), device, 0, 32)
        bulk.append((edge, halo_send.at[2, r]))

    def eliminate_unit(slot, prev, steps=range(4)):
        for kk in steps:
            k, under = at(slot, kk), at(slot, kk - 1) if kk > 0 else at(slot - 1, 3)
            prev = (1024.0 * (eta_m[under, :] + eta_m[k, :]) * inv_m[k, :]) * prev
            val_m[k, :] = prev
        return prev

    first = inv_m[0:8, :]
    val_m[0:8, :] = first
    lax.fori_loop(1, SLOTS, eliminate_unit, eliminate_unit(0, first, range(1, 4)))

    def substitute_unit(i, following):
        for kk in reversed(range(4)):
            k = at(SLOTS - 1 - i, kk)
            following = val_m[k, :] - ratio_m[k, :] * following
            val_m[k, :] = following
        return following

    lax.fori_loop(0, SLOTS, substitute_unit, zero)
    total = [zero] * 8
    for kk in range(4):
        for c in range(2):
            rows = [[am[pl.ds(kk * 8 + c * 4 + t * 2 + r, 8, stride=SLAB), :] for t in range(2)] for r in range(2)]
            for r in range(2):
                rows[r].append(rim_x[pl.ds(kk * 8 + c * 2 + r, 8, stride=SLAB), :])
            for r in range(2):
                right, left = ahead(rows[r]), behind(rows[r])
                for t in range(2):
                    s = c * 4 + t * 2 + r
                    weight = val_m[pl.ds(kk * 8 + s, 8, stride=SLAB), :]
                    east, west, north, south = [faces[kk, (r * 2 + t) * 4 + i] for i in range(4)]
                    if r == 0:
                        along, outer = east * rows[1][t], west * has_below
                    else:
                        along, outer = west * rows[0][t], east * has_above
                    across = north * right[t] + south * left[t]
                    value = 4.0 * along + across if c == 0 else along + 4.0 * across
                    total[s] = total[s] + weight * value
                    cross[kk, s] = weight * (4.0 * outer if c == 0 else outer)
    ahead_part = val_m[top, :] * source[0]

    arrived(aup, halo_recv.at[2, 0])
    arrived(adn, halo_recv.at[2, 1])
    for s in range(8):
        edge = adn if s % 2 == 0 else aup
        for kk in range(4):
            total[s] = total[s] + cross[kk, s] * edge[pl.ds(kk * 32 + s // 2, 8, stride=4), :]
        flip[s * 8:s * 8 + 8, :] = total[s]
    bottom = ahead_part
    for i in range(8):
        bottom = bottom + flip[pl.ds(i, 8, stride=8), :]
    bottom = jnp.where(ice[0], bottom, 0.0)

    product = w2[0:8, :] * bottom
    gradient = -bed[0][0:4, :] * (product[0:4, :] + product[4:8, :])
    grad[...] = gradient
    remote(grad, grad_in, grad_send, grad_recv, (bm, bl))

    lane1 = lax.broadcasted_iota(jnp.int32, (1, 128), 1)
    grad_row = jnp.sum(gradient * gradient, axis=0, keepdims=True)
    fit_row = jnp.sum(0.5 * mismatch[0] * mismatch[0], axis=0, keepdims=True)
    grad_row = grad_row + pltpu.roll(grad_row, 64, 1)
    fit_row = fit_row + pltpu.roll(fit_row, 64, 1)
    row = jnp.where(lane1 < 64, grad_row, fit_row)
    for number, (me, others, peer, row_ref, sum_ref, send_sem, recv_sem) in enumerate(stages):
        row_ref[...] = row
        sum_ref[me] = row
        for i, other in enumerate(others):
            remote(row_ref, sum_ref.at[me], send_sem.at[i], recv_sem.at[me], peer(other))
        if number == 0:
            for l in range(SLOTS):
                remote(
                    w2.at[l * SLAB:l * SLAB + 32], vel_in.at[pl.ds(pl.multiple_of(bl * SLAB, 8), 32)],
                    vel_send.at[l], vel_recv.at[bl], holders[l],
                )
        else:
            for l in range(SLOTS):
                arrived(vel_in.at[l * SLAB:l * SLAB + 32], vel_recv.at[l])
            for c in range(2):
                for kk in range(4):
                    for s in range(4):
                        piece = vel_in[pl.ds(kk * 8 + c * 4 + s, 8, stride=SLAB), :]
                        vout[pl.ds((c * 4 + kk) * 32 + s, 8, stride=4), :] = piece
        if number == 1:
            for copy in sends:
                copy.wait_send()
            bulk += [(w0, halo_send.at[0, i]) for i in range(2)]
            for src, sem in bulk:
                arrived(src, sem)
        for other in reversed(others):
            arrived(sum_ref.at[other], recv_sem.at[other])
        parts = [sum_ref[i] for i in range(32)]
        while len(parts) > 1:
            parts = [parts[i] + parts[i + 1] for i in range(0, len(parts), 2)]
        row = parts[0]

    grad_total = jnp.sum(jnp.where(lane1 < 64, row, 0.0))
    fit_total = jnp.sum(jnp.where(lane1 < 64, 0.0, row))
    misfit_out[...] = jnp.full((1, 128), fit_total, f32) / COLUMNS
    arrived(grad_in, grad_recv)
    scale = jnp.sqrt(jnp.full((4, 128), grad_total, f32) / COLUMNS + 1e-06)
    fric_out[...] = logf[...] - step_size * grad_in[...] / scale


def hand_over(out, fric, misfit, out_hbm, fric_hbm, misfit_hbm, sem):
    copies = [
        pltpu.make_async_copy(src, dst, sem.at[i])
        for i, (src, dst) in enumerate(((out, out_hbm), (fric, fric_hbm), (misfit, misfit_hbm)))
    ]
    for copy in copies:
        copy.start()
    for copy in copies:
        copy.wait()


def on_device(velocity_init, driving, observed, log_friction, ice_mask):
    vel = velocity_init.reshape(2, 4, 2, 16, 128).transpose(0, 1, 3, 2, 4).reshape(256, 128)

    def tiles(a, lead):
        b = a.reshape(lead, 2, 2, 128).transpose(0, 2, 1, 3)
        return b.reshape(lead * 4, 128)

    full, half, slab = (256, 128), (128, 128), (SLOTS * SLAB, 128)
    vm = lambda shape: pltpu.VMEM(shape, f32)
    dma = pltpu.SemaphoreType.DMA
    scratch = [vm((272, 128)), vm((8, 128)), vm((8, 128)), vm((4, 128)), pltpu.VMEM((4, 128), jnp.int32)]
    scratch += [vm(slab), vm((24, 128)), vm((3, 24, 128))]
    scratch += [vm(slab)] * 8 + [vm(half)] * 4
    scratch += [vm(slab)] * 13 + [vm((GROUPS, 16, 8, 128)), vm((GROUPS, 8, 8, 128)), vm((64, 128))]
    scratch += [vm(slab), vm((4, 128)), vm((4, 128))]
    scratch += [vm((1, 128))] * 2 + [vm((32, 1, 128))] * 2
    scratch += [dma((5,)), dma((8,)), dma((8,)), dma((3,)), dma((3,)), dma((3, 2)), dma((3, 2))]
    scratch += [dma((8,)), dma((8,)), dma, dma] + [dma((32,))] * 4 + [pltpu.SemaphoreType.REGULAR((6,))]
    anywhere = pl.BlockSpec(memory_space=pl.ANY)
    out, fric, misfit = pl.pallas_call(
        kernel,
        out_shape=(
            pltpu.VMEM(full, f32),
            pltpu.VMEM((4, 128), f32),
            pltpu.VMEM((1, 128), f32),
        ),
        in_specs=[anywhere] * 5,
        out_specs=(
            pl.BlockSpec(memory_space=pltpu.VMEM),
            pl.BlockSpec(memory_space=pltpu.VMEM),
            pl.BlockSpec(memory_space=pltpu.VMEM),
        ),
        scratch_shapes=scratch,
        compiler_params=pltpu.CompilerParams(collective_id=0, has_side_effects=True),
    )(vel, tiles(driving, 2), tiles(observed, 2), tiles(log_friction, 1), tiles(ice_mask, 1))
    out, fric, misfit = pl.pallas_call(
        hand_over,
        out_shape=(
            jax.ShapeDtypeStruct(full, f32),
            jax.ShapeDtypeStruct((4, 128), f32),
            jax.ShapeDtypeStruct((1, 128), f32),
        ),
        in_specs=[pl.BlockSpec(memory_space=pltpu.VMEM)] * 3,
        out_specs=(anywhere,) * 3,
        scratch_shapes=[dma((3,))],
    )(*(pltpu.with_memory_space_constraint(a, pltpu.VMEM) for a in (out, fric, misfit)))
    velocity = out.reshape(2, 4, 16, 2, 128).transpose(0, 1, 3, 2, 4).reshape(2, 4, 2, 2048)
    fric = fric.reshape(2, 2, 128).transpose(1, 0, 2).reshape(2, 256)
    return velocity, fric, misfit[0, 0]


def solution(mesh):
    in_specs = (
        P(None, "layer", "map", None),
        P(None, "map", "layer"),
        P(None, "map", "layer"),
        P("map", "layer"),
        P("map", "layer"),
    )
    out_specs = (P(None, "layer", "map", None), P("map", "layer"), P())
    return jax.shard_map(on_device, mesh=mesh, in_specs=in_specs, out_specs=out_specs, check_vma=False)
```

```python
import jax
import jax.numpy as jnp
from jax import lax
from jax.experimental import pallas as pl
from jax.experimental.pallas import tpu as pltpu
from jax.sharding import PartitionSpec as P

strain_floor = 0.1
step_size = 0.5
LAYERS = 32
SLOTS = 8
BLOCKS = 128
GROUPS = 4
COLUMNS = 256 * 2048
MESH = pl.DeviceIdType.MESH
f32 = jnp.float32

SLAB = 40


def place(m):
    return lax.div(m, 8), lax.rem(lax.div(m, 2), 4), lax.rem(m, 2)


def device_at(x, y, z, core):
    return ((z * 4 + lax.rem(y, 4)) * 2 + core, x * 2 + lax.div(y, 4))


def owner_of(m, l):
    z, y_lo, core = place(m)
    y = lax.rem(l, 2) * 4 + y_lo
    odd = lax.rem(z, 2)
    return device_at(lax.div(l, 2), lax.rem((1 - odd) * (y + 2) + odd * (13 - y), 8), z, core)


def block_of(x, y, z, core):
    odd = lax.rem(z, 2)
    return device_at(x, lax.rem((1 - odd) * (y + 6) + odd * (13 - y), 8), z, core)


def kernel(
    vel_hbm, drv_hbm, obs_hbm, logf_hbm, mask_hbm,
    vout, fric_out, misfit_out,
    vin, drv, obs, logf, mask, stage, small, small_in,
    w0, w1, w2, dn0, up0, dn1, up1, am, adn, aup, alow, ahigh,
    eta_m, eta_r, diag_m, diag_r, rhs_m, rhs_r, ratio_m, ratio_r, val_m, val_r, inv_m, inv_r, rim_x, faces, cross, flip,
    vel_in, grad, grad_in, row1, row2, sum1, sum2,
    load_sem, a2a_send, a2a_recv, small_send, small_recv, halo_send, halo_recv,
    vel_send, vel_recv, grad_send, grad_recv, s1_send, s1_recv, s2_send, s2_recv, token,
):
    loads = [
        pltpu.make_async_copy(src, dst, load_sem.at[i])
        for i, (src, dst) in enumerate(
            ((vel_hbm, vin.at[8:264]), (drv_hbm, drv), (obs_hbm, obs), (logf_hbm, logf), (mask_hbm, mask))
        )
    ]
    for load in loads:
        load.start()

    M = lax.axis_index("map")
    L = lax.axis_index("layer")
    z, y_lo, core = place(M)
    x = lax.div(L, 2)
    y = lax.rem(L, 2) * 4 + y_lo
    bm, bl = block_of(x, y, z, core)
    below = owner_of(lax.rem(bm + BLOCKS - 1, BLOCKS), bl)
    above = owner_of(lax.rem(bm + 1, BLOCKS), bl)
    own_map, own_half = owner_of(M, jnp.int32(0))
    flip_half = 1 - 2 * own_half

    def owner_in_row(column, half):
        return own_map, column * 2 + own_half + half * flip_half

    owners = [owner_in_row(jnp.int32(column), half) for column in range(4) for half in range(2)]
    holders = [(bm, jnp.int32(l)) for l in range(SLOTS)]

    def peer_z(j):
        return device_at(x, y, lax.div(j, 2), lax.rem(j, 2))

    def peer_xy(j):
        return device_at(lax.div(j, 8), lax.rem(j, 8), z, core)

    ring_z = sorted(((dz, dc) for dz in range(16) for dc in range(2)), key=lambda d: -min(d[0], 16 - d[0]) - d[1] / 2)[:-1]
    ring_xy = sorted(((dx, dy) for dx in range(4) for dy in range(8)), key=lambda d: -min(d[0], 4 - d[0]) - min(d[1], 8 - d[1]))[:-1]
    zs = [lax.rem(z + dz, 16) for dz in range(16)]
    xs = [lax.rem(x + dx, 4) for dx in range(4)]
    ys = [lax.rem(y + dy, 8) for dy in range(8)]
    stages = (
        (z * 2 + core, [zs[dz] * 2 + (1 - core if dc else core) for dz, dc in ring_z], peer_z, row1, sum1, s1_send, s1_recv),
        (x * 8 + y, [xs[dx] * 8 + ys[dy] for dx, dy in ring_xy], peer_xy, row2, sum2, s2_send, s2_recv),
    )

    def along_z(far):
        return device_at(x, y, lax.rem(far, 16), core)

    partners = owners + holders + [below, above, along_z(z + 1), along_z(z + 15)]
    barrier = pltpu.get_barrier_semaphore()
    for partner in partners:
        pl.semaphore_signal(barrier, inc=1, device_id=partner, device_id_type=MESH)

    for load in loads[1:]:
        load.wait()
    small[0:8, :] = drv[...]
    small[8:16, :] = obs[...]
    small[16:20, :] = jnp.exp(logf[...]) * (mask[...] == 1).astype(f32)
    small[20:24, :] = (mask[...] != 0).astype(f32)
    loads[0].wait()

    lane2 = lax.broadcasted_iota(jnp.int32, (2, 128), 1)
    lane8 = lax.broadcasted_iota(jnp.int32, (8, 128), 1)
    row8 = lax.broadcasted_iota(jnp.int32, (8, 128), 0)
    zero = jnp.zeros((8, 128), f32)

    def turn(v):
        return pltpu.roll(v, 64, 1)

    def pack(right_a, left_a, right_b, left_b):
        low = jnp.where(lane8 < 32, right_a, turn(left_a))
        return jnp.where(lane8 < 64, low, jnp.where(lane8 < 96, turn(right_b), left_b))

    for c in range(2):
        for kk in range(4):
            for s in range(4):
                stage[pl.ds(kk * 8 + c * 4 + s, 8, stride=SLAB), :] = vin[pl.ds(8 + (c * 4 + kk) * 32 + s, 8, stride=4), :]
        for q in range(2):
            for r in range(2):
                sides = []
                for kk in (2 * q, 2 * q + 1):
                    first = 8 + (c * 4 + kk) * 32 + r
                    sides.append(jnp.where(row8 < SLOTS - 1, vin[pl.ds(first + 4, 8, stride=4), :], 0.0))
                    sides.append(jnp.where(row8 > 0, vin[pl.ds(first - 2, 8, stride=4), :], 0.0))
                stage[pl.ds(32 + q * 4 + c * 2 + r, 8, stride=SLAB), :] = pack(*sides)

    pl.semaphore_wait(barrier, len(partners))

    def give_tokens(level):
        for way, far in ((0, z + (1 << level)), (1, z + 16 - (1 << level))):
            pl.semaphore_signal(token.at[level * 2 + way], inc=1, device_id=along_z(far), device_id_type=MESH)

    def take_tokens(level):
        for way in range(2):
            pl.semaphore_wait(token.at[level * 2 + way], 1)

    give_tokens(0)
    sends = []

    def remote(src, dst, send_sem, recv_sem, device):
        copy = pltpu.make_async_remote_copy(
            src_ref=src, dst_ref=dst, send_sem=send_sem, recv_sem=recv_sem, device_id=device, device_id_type=MESH
        )
        copy.start()
        sends.append(copy)

    bulk = []

    def pieces(src, dst, count, index, device, first, length):
        size = src.shape[0] // count
        for i in reversed(range(count)):
            rows = pl.ds(i * size + first, length)
            pltpu.make_async_remote_copy(
                src_ref=src.at[rows], dst_ref=dst.at[rows], send_sem=halo_send.at[index],
                recv_sem=halo_recv.at[index], device_id=device, device_id_type=MESH,
            ).start()

    def arrived(ref, sem):
        pltpu.make_async_copy(ref, ref, sem).wait()

    rows = pl.ds(pl.multiple_of(L * SLAB, 8), SLAB)
    def slots_by_x(order):
        return [lax.rem(x + dx, 4) * 2 + half for dx in order for half in range(2)]

    for dx in (2, 1, 3, 0):
        column = lax.rem(x + dx, 4)
        for half in range(2):
            l = column * 2 + half
            part = pl.ds(pl.multiple_of(l * SLAB, 8), SLAB)
            remote(stage.at[part], w0.at[rows], a2a_send.at[l], a2a_recv.at[L], owner_in_row(column, half))
    for side in range(3):
        target = owner_of(M, lax.rem(L + SLOTS + 1 - side, SLOTS))
        remote(small, small_in.at[side], small_send.at[side], small_recv.at[side], target)

    take_tokens(0)
    give_tokens(1)
    for l in slots_by_x((0, 1, 3, 2)):
        rows = pl.ds(pl.multiple_of(l * SLAB, 8), SLAB)
        arrived(w0.at[rows], a2a_recv.at[l])
        for i, (device, land) in enumerate(((below, up0), (above, dn0))):
            pltpu.make_async_remote_copy(
                src_ref=w0.at[rows], dst_ref=land.at[rows], send_sem=halo_send.at[0, i],
                recv_sem=halo_recv.at[0, i], device_id=device, device_id_type=MESH,
            ).start()

    take_tokens(1)
    give_tokens(2)
    for side in range(3):
        arrived(small_in.at[side], small_recv.at[side])
    has_left = (bl > 0).astype(f32)
    has_right = (bl < SLOTS - 1).astype(f32)
    has_below = (bm > 0).astype(f32)
    has_above = (bm < BLOCKS - 1).astype(f32)

    def double(rows):
        return jnp.concatenate([rows, rows], 0)

    def rim_rows(start, comps):
        parts = []
        for c in range(comps):
            at = start + 4 * c
            parts.append(jnp.where(lane2 < 64, small_in[2, at:at + 2, :] * has_right, small_in[0, at + 2:at + 4, :] * has_left))
        if comps == 1:
            parts = parts * 2
        return double(jnp.concatenate(parts, 0))

    drive = (small_in[1, 0:8, :], rim_rows(0, 2))
    seen = (small_in[1, 8:16, :], rim_rows(8, 2))
    bed = (double(small_in[1, 16:20, :]), rim_rows(16, 1))
    ice = (double(small_in[1, 20:24, :]) > 0.5, rim_rows(20, 1) > 0.5)

    def ahead(tiles):
        turned = [pltpu.roll(t, 127, 1) for t in tiles]
        return [jnp.where(lane8 == 127, turned[(i + 1) % 3], turned[i]) for i in range(3)]

    def behind(tiles):
        turned = [pltpu.roll(t, 1, 1) for t in tiles]
        return [jnp.where(lane8 == 0, turned[(i + 2) % 3], turned[i]) for i in range(3)]

    def load_tiles(slab, c, r, kk, packed):
        tiles = [slab[pl.ds(kk * 8 + c * 4 + t * 2 + r, 8, stride=SLAB), :] for t in range(2)]
        return tiles + [packed[kk % 2]]

    def unpack(slab, c, r, q):
        v = slab[pl.ds(32 + q * 4 + c * 2 + r, 8, stride=SLAB), :]
        turned = turn(v)
        return jnp.where(lane8 < 64, v, turned), jnp.where(lane8 < 64, turned, v)

    def store_tile(main, rim, kk, c, t, r, value):
        if t < 2:
            main[pl.ds(kk * 8 + c * 4 + t * 2 + r, 8, stride=SLAB), :] = value
        else:
            rim[pl.ds(kk * 8 + c * 2 + r, 8, stride=SLAB), :] = value

    def scaled(tiles, factor):
        return [t * factor for t in tiles]

    def forward_terms(own, low, high):
        for q in range(2):
            rims = [[unpack(slab, c, r, q) for slab in (low, own, high) for r in range(2)] for c in range(2)]
            for kk in (2 * q, 2 * q + 1):
                group(own, low, high, kk, rims)

    def group(own, low, high, kk, rims):
        w = []
        for c in range(2):
            rows = [scaled(load_tiles(low, c, r, kk, rims[c][r]), has_below) for r in range(2)]
            rows += [load_tiles(own, c, r, kk, rims[c][2 + r]) for r in range(2)]
            rows += [scaled(load_tiles(high, c, r, kk, rims[c][4 + r]), has_above) for r in range(2)]
            w.append(rows)
        right = [[ahead(w[c][r]) for r in range(1, 5)] for c in range(2)]
        left = [[behind(w[c][r]) for r in range(1, 5)] for c in range(2)]
        eta = []
        for r in range(4):
            tiles = []
            for t in range(3):
                u_x = (w[0][r + 2][t] - w[0][r][t]) * 0.5
                v_x = (w[1][r + 2][t] - w[1][r][t]) * 0.5
                u_y = (right[0][r][t] - left[0][r][t]) * 0.5
                v_y = (right[1][r][t] - left[1][r][t]) * 0.5
                shear = u_y + v_x
                rate = u_x * u_x + v_y * v_y + u_x * v_y + 0.25 * shear * shear
                tiles.append(jnp.exp(jnp.log(strain_floor + rate) * (-1.0 / 3.0)))
            eta.append(tiles)
        for r in range(2):
            eta_right, eta_left = ahead(eta[r + 1]), behind(eta[r + 1])
            for t in range(3):
                centre = eta[r + 1][t]
                east = 0.5 * (centre + eta[r + 2][t])
                west = 0.5 * (centre + eta[r][t])
                north = 0.5 * (centre + eta_right[t])
                south = 0.5 * (centre + eta_left[t])
                along, across = east + west, north + south
                if t < 2:
                    for i, face in enumerate((east, west, north, south)):
                        faces[kk, (r * 2 + t) * 4 + i] = face
                u, v = w
                sum_u = (
                    4.0 * (east * u[r + 3][t] + west * u[r + 1][t])
                    + north * right[0][r + 1][t] + south * left[0][r + 1][t]
                )
                sum_v = (
                    east * v[r + 3][t] + west * v[r + 1][t]
                    + 4.0 * (north * right[1][r + 1][t] + south * left[1][r + 1][t])
                )
                store_tile(eta_m, eta_r, kk, 0, t, r, centre)
                store_tile(eta_m, eta_r, kk, 1, t, r, centre)
                store_tile(diag_m, diag_r, kk, 0, t, r, 4.0 * along + across)
                store_tile(diag_m, diag_r, kk, 1, t, r, along + 4.0 * across)
                store_tile(rhs_m, rhs_r, kk, 0, t, r, sum_u)
                store_tile(rhs_m, rhs_r, kk, 1, t, r, sum_v)

    pairs = (
        (eta_m, diag_m, rhs_m, ratio_m, val_m, inv_m),
        (eta_r, diag_r, rhs_r, ratio_r, val_r, inv_r),
    )

    def at(slot, kk):
        return pl.ds(pl.multiple_of(slot * SLAB + kk * 8, 8), 8)

    def solve(out):
        def eliminate(slot, carry, last=False):
            for kk in range(4):
                new = []
                for part in range(2):
                    eta, diag, rhs, ratio, val, inv = pairs[part]
                    lower, ratio_prev, val_prev, pad = carry[part]
                    k = at(slot, kk)
                    if last and kk == 3:
                        upper = zero
                    else:
                        upper = 1024.0 * (eta[k, :] + eta[at(slot, kk + 1) if kk < 3 else at(slot + 1, 0), :])
                    inverse = 1.0 / (((lower + upper + pad) + diag[k, :]) + lower * ratio_prev)
                    ratio_now = -upper * inverse
                    val_now = (drive[part] + rhs[k, :] + lower * val_prev) * inverse
                    ratio[k, :] = ratio_now
                    val[k, :] = val_now
                    inv[k, :] = inverse
                    new.append((upper, ratio_now, val_now, zero))
                carry = tuple(new)
            return carry

        carry = tuple((zero, zero, zero, bed[part]) for part in range(2))
        carry = lax.fori_loop(0, SLOTS - 1, eliminate, carry, unroll=True)
        eliminate(SLOTS - 1, carry, last=True)

        def substitute(i, following):
            slot = SLOTS - 1 - i
            for kk in reversed(range(4)):
                k = at(slot, kk)
                new = []
                for part, to in enumerate((out, rim_x)):
                    ratio, val = pairs[part][3], pairs[part][4]
                    now = val[k, :] - ratio[k, :] * following[part]
                    to[k, :] = jnp.where(ice[part], now, 0.0)
                    new.append(now)
                following = tuple(new)
            return following

        lax.fori_loop(0, SLOTS, substitute, (zero, zero), unroll=True)

    def pack_rims(out):
        for q in range(2):
            for s in range(4):
                a = rim_x[pl.ds(2 * q * 8 + s, 8, stride=SLAB), :]
                b = rim_x[pl.ds((2 * q + 1) * 8 + s, 8, stride=SLAB), :]
                out[pl.ds(32 + q * 4 + s, 8, stride=SLAB), :] = pack(a, a, b, b)

    for i, land in enumerate((up0, dn0)):
        arrived(land, halo_recv.at[0, i])
    forward_terms(w0, dn0, up0)
    solve(w1)
    for i, (device, land) in enumerate(((below, up1), (above, dn1))):
        pieces(w1, land, SLOTS, (1, i), device, 0, 32)
        bulk.append((w1, halo_send.at[1, i]))
    pack_rims(w1)
    for i, (device, land) in enumerate(((below, up1), (above, dn1))):
        pieces(w1, land, SLOTS, (1, i), device, 32, 8)

    for i, land in enumerate((up1, dn1)):
        arrived(land, halo_recv.at[1, i])
    forward_terms(w1, dn1, up1)
    solve(w2)
    take_tokens(2)

    top = pl.ds((SLOTS - 1) * SLAB + 24, 8)
    tops = (w2[top, :], rim_x[top, :])
    mismatch = [jnp.where(ice[part], tops[part] - seen[part], 0.0) for part in range(2)]
    source = [float(LAYERS) * mismatch[part] for part in range(2)]
    starts = tuple(source[part] * pairs[part][5][top, :] for part in range(2))
    adjoints = (am, rim_x)
    for part in range(2):
        adjoints[part][top, :] = jnp.where(ice[part], starts[part], 0.0)

    def substitute_first(slot, following, steps=range(4)):
        for kk in reversed(steps):
            k = at(slot, kk)
            new = []
            for part in range(2):
                now = -pairs[part][3][k, :] * following[part]
                adjoints[part][k, :] = jnp.where(ice[part], now, 0.0)
                new.append(now)
            following = tuple(new)
        return following

    following = substitute_first(SLOTS - 1, starts, range(3))
    lax.fori_loop(1, SLOTS, lambda i, carry: substitute_first(SLOTS - 1 - i, carry), following)
    for r, (edge, land, device) in enumerate(((alow, aup, below), (ahigh, adn, above))):
        for s in range(4):
            for j in range(GROUPS):
                edge[pl.ds(j * 32 + s, 8, stride=4), :] = am[pl.ds(j * 8 + s * 2 + r, 8, stride=SLAB), :]
        pieces(edge, land, 4, (2, r), device, 0, 32)
        bulk.append((edge, halo_send.at[2, r]))

    def eliminate_unit(slot, prev, steps=range(4)):
        for kk in steps:
            k, under = at(slot, kk), at(slot, kk - 1) if kk > 0 else at(slot - 1, 3)
            prev = (1024.0 * (eta_m[under, :] + eta_m[k, :]) * inv_m[k, :]) * prev
            val_m[k, :] = prev
        return prev

    first = inv_m[0:8, :]
    val_m[0:8, :] = first
    lax.fori_loop(1, SLOTS, eliminate_unit, eliminate_unit(0, first, range(1, 4)))

    def substitute_unit(i, following):
        for kk in reversed(range(4)):
            k = at(SLOTS - 1 - i, kk)
            following = val_m[k, :] - ratio_m[k, :] * following
            val_m[k, :] = following
        return following

    lax.fori_loop(0, SLOTS, substitute_unit, zero)
    total = [zero] * 8
    for kk in range(4):
        for c in range(2):
            rows = [[am[pl.ds(kk * 8 + c * 4 + t * 2 + r, 8, stride=SLAB), :] for t in range(2)] for r in range(2)]
            for r in range(2):
                rows[r].append(rim_x[pl.ds(kk * 8 + c * 2 + r, 8, stride=SLAB), :])
            for r in range(2):
                right, left = ahead(rows[r]), behind(rows[r])
                for t in range(2):
                    s = c * 4 + t * 2 + r
                    weight = val_m[pl.ds(kk * 8 + s, 8, stride=SLAB), :]
                    east, west, north, south = [faces[kk, (r * 2 + t) * 4 + i] for i in range(4)]
                    if r == 0:
                        along, outer = east * rows[1][t], west * has_below
                    else:
                        along, outer = west * rows[0][t], east * has_above
                    across = north * right[t] + south * left[t]
                    value = 4.0 * along + across if c == 0 else along + 4.0 * across
                    total[s] = total[s] + weight * value
                    cross[kk, s] = weight * (4.0 * outer if c == 0 else outer)
    ahead_part = val_m[top, :] * source[0]

    arrived(aup, halo_recv.at[2, 0])
    arrived(adn, halo_recv.at[2, 1])
    for s in range(8):
        edge = adn if s % 2 == 0 else aup
        for kk in range(4):
            total[s] = total[s] + cross[kk, s] * edge[pl.ds(kk * 32 + s // 2, 8, stride=4), :]
        flip[s * 8:s * 8 + 8, :] = total[s]
    bottom = ahead_part
    for i in range(8):
        bottom = bottom + flip[pl.ds(i, 8, stride=8), :]
    bottom = jnp.where(ice[0], bottom, 0.0)

    product = w2[0:8, :] * bottom
    gradient = -bed[0][0:4, :] * (product[0:4, :] + product[4:8, :])
    grad[...] = gradient
    remote(grad, grad_in, grad_send, grad_recv, (bm, bl))

    lane1 = lax.broadcasted_iota(jnp.int32, (1, 128), 1)
    grad_row = jnp.sum(gradient * gradient, axis=0, keepdims=True)
    fit_row = jnp.sum(0.5 * mismatch[0] * mismatch[0], axis=0, keepdims=True)
    grad_row = grad_row + pltpu.roll(grad_row, 64, 1)
    fit_row = fit_row + pltpu.roll(fit_row, 64, 1)
    row = jnp.where(lane1 < 64, grad_row, fit_row)
    for number, (me, others, peer, row_ref, sum_ref, send_sem, recv_sem) in enumerate(stages):
        row_ref[...] = row
        sum_ref[me] = row
        for i, other in enumerate(others):
            remote(row_ref, sum_ref.at[me], send_sem.at[i], recv_sem.at[me], peer(other))
        if number == 0:
            for l in range(SLOTS):
                remote(
                    w2.at[l * SLAB:l * SLAB + 32], vel_in.at[pl.ds(pl.multiple_of(bl * SLAB, 8), 32)],
                    vel_send.at[l], vel_recv.at[bl], holders[l],
                )
        else:
            for l in range(SLOTS):
                arrived(vel_in.at[l * SLAB:l * SLAB + 32], vel_recv.at[l])
            for c in range(2):
                for kk in range(4):
                    for s in range(4):
                        piece = vel_in[pl.ds(kk * 8 + c * 4 + s, 8, stride=SLAB), :]
                        vout[pl.ds((c * 4 + kk) * 32 + s, 8, stride=4), :] = piece
        if number == 1:
            for copy in sends:
                copy.wait_send()
            bulk += [(w0, halo_send.at[0, i]) for i in range(2)]
            for src, sem in bulk:
                arrived(src, sem)
        for other in reversed(others):
            arrived(sum_ref.at[other], recv_sem.at[other])
        parts = [sum_ref[i] for i in range(32)]
        while len(parts) > 1:
            parts = [parts[i] + parts[i + 1] for i in range(0, len(parts), 2)]
        row = parts[0]

    grad_total = jnp.sum(jnp.where(lane1 < 64, row, 0.0))
    fit_total = jnp.sum(jnp.where(lane1 < 64, 0.0, row))
    misfit_out[...] = jnp.full((1, 128), fit_total, f32) / COLUMNS
    arrived(grad_in, grad_recv)
    scale = jnp.sqrt(jnp.full((4, 128), grad_total, f32) / COLUMNS + 1e-06)
    fric_out[...] = logf[...] - step_size * grad_in[...] / scale


def hand_over(out, fric, misfit, out_hbm, fric_hbm, misfit_hbm, sem):
    copies = [
        pltpu.make_async_copy(src, dst, sem.at[i])
        for i, (src, dst) in enumerate(((out, out_hbm), (fric, fric_hbm), (misfit, misfit_hbm)))
    ]
    for copy in copies:
        copy.start()
    for copy in copies:
        copy.wait()


def on_device(velocity_init, driving, observed, log_friction, ice_mask):
    vel = velocity_init.reshape(2, 4, 2, 16, 128).transpose(0, 1, 3, 2, 4).reshape(256, 128)

    def tiles(a, lead):
        b = a.reshape(lead, 2, 2, 128).transpose(0, 2, 1, 3)
        return b.reshape(lead * 4, 128)

    full, half, slab = (256, 128), (128, 128), (SLOTS * SLAB, 128)
    vm = lambda shape: pltpu.VMEM(shape, f32)
    dma = pltpu.SemaphoreType.DMA
    scratch = [vm((272, 128)), vm((8, 128)), vm((8, 128)), vm((4, 128)), pltpu.VMEM((4, 128), jnp.int32)]
    scratch += [vm(slab), vm((24, 128)), vm((3, 24, 128))]
    scratch += [vm(slab)] * 8 + [vm(half)] * 4
    scratch += [vm(slab)] * 13 + [vm((GROUPS, 16, 8, 128)), vm((GROUPS, 8, 8, 128)), vm((64, 128))]
    scratch += [vm(slab), vm((4, 128)), vm((4, 128))]
    scratch += [vm((1, 128))] * 2 + [vm((32, 1, 128))] * 2
    scratch += [dma((5,)), dma((8,)), dma((8,)), dma((3,)), dma((3,)), dma((3, 2)), dma((3, 2))]
    scratch += [dma((8,)), dma((8,)), dma, dma] + [dma((32,))] * 4 + [pltpu.SemaphoreType.REGULAR((6,))]
    anywhere = pl.BlockSpec(memory_space=pl.ANY)
    out, fric, misfit = pl.pallas_call(
        kernel,
        out_shape=(
            pltpu.VMEM(full, f32),
            pltpu.VMEM((4, 128), f32),
            pltpu.VMEM((1, 128), f32),
        ),
        in_specs=[anywhere] * 5,
        out_specs=(
            pl.BlockSpec(memory_space=pltpu.VMEM),
            pl.BlockSpec(memory_space=pltpu.VMEM),
            pl.BlockSpec(memory_space=pltpu.VMEM),
        ),
        scratch_shapes=scratch,
        compiler_params=pltpu.CompilerParams(collective_id=0, has_side_effects=True),
    )(vel, tiles(driving, 2), tiles(observed, 2), tiles(log_friction, 1), tiles(ice_mask, 1))
    out, fric, misfit = pl.pallas_call(
        hand_over,
        out_shape=(
            jax.ShapeDtypeStruct(full, f32),
            jax.ShapeDtypeStruct((4, 128), f32),
            jax.ShapeDtypeStruct((1, 128), f32),
        ),
        in_specs=[pl.BlockSpec(memory_space=pltpu.VMEM)] * 3,
        out_specs=(anywhere,) * 3,
        scratch_shapes=[dma((3,))],
    )(*(pltpu.with_memory_space_constraint(a, pltpu.VMEM) for a in (out, fric, misfit)))
    velocity = out.reshape(2, 4, 16, 2, 128).transpose(0, 1, 3, 2, 4).reshape(2, 4, 2, 2048)
    fric = fric.reshape(2, 2, 128).transpose(1, 0, 2).reshape(2, 256)
    return velocity, fric, misfit[0, 0]


def solution(mesh):
    in_specs = (
        P(None, "layer", "map", None),
        P(None, "map", "layer"),
        P(None, "map", "layer"),
        P("map", "layer"),
        P("map", "layer"),
    )
    out_specs = (P(None, "layer", "map", None), P("map", "layer"), P())
    return jax.shard_map(on_device, mesh=mesh, in_specs=in_specs, out_specs=out_specs, check_vma=False)
```
